128 devices in a mesh: row: 8 (over z, y_lo), col: 16 (over y_hi, x, core).
Axes of the slice: x: 4, y: 4 (y_hi: 2, y_lo: 2; y = y_hi * 2 + y_lo), z: 4, core: 2. Of those that a mesh axis runs over, the one named last changes fastest.
Arguments:
- stiffness: float32 [4, 8, 512, 2, 16, 512], P(None, 'row', None, None, 'col'), may hold values from -7 to 7
- lower_panel: float32 [4, 8, 512, 512], P(None, 'row'), may hold values from -0.25 to 0.25
- diag_inverse: float32 [512, 512], replicated, as said below
Outputs:
- reduced: float32 [4, 8, 512, 2, 16, 512], P(None, 'row', None, None, 'col')
The draws below stay inside these ranges and needn't reach their ends.
Inputs may be any that keep to these rules, and one draw needn't show every extreme that they name: diag_inverse is lower triangular with a positive diagonal.
All inputs are finite; a program needn't handle non-finite values.
Results may differ from the reference program's by a relative error of at most 0.000062.
Values sent between devices are 32-bit elements; how exact they have to be, the bound alone decides.
A program may use at most 128 MiB of HBM per device.

```python
import jax
import jax.numpy as jnp
from jax import lax

NB = 512
ORDER = 16384
BR = 4
BC = 2
N_ROW = 8
N_COL = 16


def draw_stiffness(key, part):
    first = jax.random.fold_in(key, 0)
    base = jnp.clip(jax.random.normal(first, (ORDER, ORDER), jnp.float32), -4.0, 4.0)
    sym = 0.5 * (base + base.T)
    return sym.reshape(BR, N_ROW, NB, BC, N_COL, NB)


def draw_diag_inverse(key, part):
    first, second = jax.random.split(key)
    diag = jnp.exp(jax.random.uniform(first, (NB,), jnp.float32, -0.7, 0.7))
    off = jax.random.normal(second, (NB, NB), jnp.float32)
    off = jnp.tril(off, -1) * (0.5 / jnp.sqrt(jnp.float32(NB)))
    return off + jnp.diag(diag)


def steps_of(rng, shape, pieces, low, top_value):
    factor_of = 1.0
    for dim, parts in pieces:
        draws = jax.random.uniform(jax.random.fold_in(jax.random.fold_in(rng, 6), dim), (parts,), jnp.float32, low / len(pieces), top_value / len(pieces))
        factor_of = factor_of * jnp.repeat(jnp.exp(draws), shape[dim] // parts).reshape((-1,) + (1,) * (len(shape) - 1 - dim))
    return factor_of


def centred(rng, extent, spread, limit, cuts=(), held_as=jnp.bfloat16):
    gain = steps_of(rng, extent, cuts, -0.22, 0.18) if cuts else 1.0
    values = jax.random.normal(rng, extent, jnp.float32) * spread * gain
    return jnp.minimum(jnp.maximum(values, -limit), limit).astype(held_as)


def setup_inputs(seed: int = 0) -> dict:
    key_list = jax.random.split(jax.random.key(seed), 4)
    return {
        "stiffness": draw_stiffness(jax.random.fold_in(key_list[3], 71), 0),
        "lower_panel": centred(key_list[1], (BR, N_ROW, NB, NB), NB ** -0.5, 0.25, ((1, 8),), jnp.float32),
        "diag_inverse": draw_diag_inverse(jax.random.fold_in(key_list[3], 71), 0),
    }


def reference(stiffness, lower_panel, diag_inverse):
    highest = lax.Precision.HIGHEST
    shape = stiffness.shape
    whole = stiffness.reshape(ORDER, ORDER)
    lower = lower_panel.reshape(ORDER, NB)
    lower = lower.at[:NB, :].set(jnp.zeros((NB, NB), jnp.float32))
    corner = whole[:NB, :NB]
    c_block = jnp.dot(jnp.dot(diag_inverse, corner, precision=highest), diag_inverse.T, precision=highest)
    panel = whole[:, :NB].at[:NB, :].set(jnp.zeros((NB, NB), jnp.float32))
    lower_c = jnp.dot(lower, c_block, precision=highest)
    w_panel = jnp.dot(panel, diag_inverse.T, precision=highest) - 0.5 * lower_c
    update = whole - jnp.dot(w_panel, lower.T, precision=highest) - jnp.dot(lower, w_panel.T, precision=highest)
    final_panel = w_panel - 0.5 * lower_c
    update = update.at[:, :NB].set(final_panel)
    update = update.at[:NB, :].set(final_panel.T)
    update = update.at[:NB, :NB].set(c_block)
    return update.reshape(shape)
```

```python
import functools

import jax
import jax.numpy as jnp
from jax import lax
from jax.experimental import pallas as pl
from jax.experimental.pallas import tpu as pltpu
from jax.sharding import PartitionSpec as P

F32, BF = jnp.float32, jnp.bfloat16
MESH = pl.DeviceIdType.MESH
NT = (((1,), (1,)), ((), ()))
NN = (((1,), (0,)), ((), ()))
PIECES = 16
CHUNKS = 8


def split(x):
    high = x.astype(BF)
    return high, (x - high.astype(F32)).astype(BF)


def dot3(ah, al, bh, bl, dims):
    dot = functools.partial(
        lax.dot_general, dimension_numbers=dims, preferred_element_type=F32
    )
    return dot(ah, bh) + dot(ah, bl) + dot(al, bh)


def gather_kernel(
    a, low, dinv, qi, lj, qj, raw, turned, dh, dl, send_sems, recv_sems, local_sems
):
    row, col = lax.axis_index("row"), lax.axis_index("col")
    z, yl = row // 2, lax.rem(row, 2)
    yh, x, k = col // 8, lax.rem(col // 2, 4), lax.rem(col, 2)
    y = 2 * yh + yl
    nb = dinv.shape[0]
    part = nb // PIECES

    def at(dx=0, dy=0, dz=0, dk=0):
        nx, ny = lax.rem(x + dx + 4, 4), lax.rem(y + dy + 4, 4)
        nz, nk = lax.rem(z + dz + 4, 4), lax.rem(k + dk, 2)
        return (2 * nz + lax.rem(ny, 2), 8 * (ny // 2) + 2 * nx + nk)

    used = {"send": 0, "recv": 0, "local": 0}
    open_sends = []

    def take(kind, count=1):
        first = used[kind]
        used[kind] += count
        return first

    def when(cond, body):
        if cond is None:
            body()
        else:
            pl.when(cond)(body)

    def send(cond, src, dst, recv, device):
        sem = take("send")

        def copy():
            return pltpu.make_async_remote_copy(
                src_ref=src,
                dst_ref=dst,
                send_sem=send_sems.at[sem],
                recv_sem=recv_sems.at[recv],
                device_id=device,
                device_id_type=MESH,
            )

        when(cond, lambda: copy().start())
        open_sends.append((cond, lambda: copy().wait_send()))

    def arrive(cond, dst, recv):
        def body():
            pltpu.make_async_remote_copy(
                src_ref=dst,
                dst_ref=dst,
                send_sem=send_sems.at[0],
                recv_sem=recv_sems.at[recv],
                device_id=at(dk=1),
                device_id_type=MESH,
            ).wait_recv()

        when(cond, body)

    barrier = pltpu.get_barrier_semaphore()

    def greet(cond, device):
        when(
            cond,
            lambda: pl.semaphore_signal(
                barrier, inc=1, device_id=device, device_id_type=MESH
            ),
        )

    neighbours = [at(dx=1), at(dx=3), at(dy=1), at(dy=3), at(dz=1), at(dz=3), at(dy=2), at(dk=1)]
    for device in neighbours:
        greet(None, device)
    greet(col != 0, (row, 0))
    greet(row != 0, (0, col))
    greet(None, (0, lax.rem(col + 8, PIECES)))
    expect = (
        len(neighbours)
        + jnp.where(col == 0, PIECES - 1, 0)
        + jnp.where(row == 0, 7 + 8, 0)
    )
    pl.semaphore_wait(barrier, expect)

    raw_recv = take("recv")
    for piece in range(1, PIECES):
        send(
            col == 0,
            a.at[:, pl.ds(piece * part, part), 0],
            raw,
            raw_recv,
            (row, piece),
        )
    own_raw = pltpu.make_async_copy(
        a.at[:, pl.ds(0, part), 0], raw, local_sems.at[take("local")]
    )
    pl.when(col == 0)(lambda: own_raw.start())

    dz = lax.rem(z - x + 4, 4)
    size = nb // CHUNKS

    def exchange(source, target):
        root = dz == 0
        mine = jnp.logical_and(root, yl == k)
        other = jnp.logical_and(root, yl != k)
        cross = take("recv", 2 * CHUNKS)
        ring = take("recv", 2 * CHUNKS)
        keep = [
            pltpu.make_async_copy(
                source.at[2 * c + yh], target.at[c], local_sems.at[take("local")]
            )
            for c in range(2)
        ]

        def rows(s):
            return pl.ds(s * size, size)

        def start():
            @pl.when(mine)
            def _():
                for copy in keep:
                    copy.start()

            for s in range(CHUNKS):
                for c, dy in ((0, 1), (1, 3)):
                    their = lax.rem(y + dy, 4) // 2
                    send(
                        mine,
                        source.at[2 * c + their, rows(s)],
                        target.at[c, rows(s)],
                        cross + c * CHUNKS + s,
                        at(dy=dy),
                    )
                    send(
                        mine,
                        source.at[2 * c + yh, rows(s)],
                        target.at[c, rows(s)],
                        ring + c * CHUNKS + s,
                        at(dz=1 if c == 0 else 3),
                    )

        def step(s):
            for c in range(2):
                here = target.at[c, rows(s)]
                arrive(other, here, cross + c * CHUNKS + s)
                arrive(dz != 0, here, ring + c * CHUNKS + s)
                last = dz == (3 if c == 0 else 1)
                send(
                    jnp.logical_and(jnp.logical_not(mine), jnp.logical_not(last)),
                    here,
                    here,
                    ring + c * CHUNKS + s,
                    at(dz=1 if c == 0 else 3),
                )

        def finish():
            @pl.when(mine)
            def _():
                for copy in keep:
                    copy.wait()

        return start, step, finish

    l_start, l_step, l_finish = exchange(low, lj)
    l_start()

    dh[...], dl[...] = split(dinv[...])
    arrive(col != 0, raw, raw_recv)
    pl.when(col == 0)(lambda: own_raw.wait())

    for b in range(4):
        rows = jnp.concatenate([raw[b, :, t, :] for t in range(4)], axis=1)
        high, lo = split(rows)
        turned[b] = dot3(high, lo, dh[...], dl[...], NT)
    turned[4] = turned[0]

    def slab(piece, count=5):
        return qi.at[pl.ds(0, count), pl.ds(pl.multiple_of(piece * part, part), part)]

    head = take("recv")
    head2 = take("recv")
    pair = take("recv")
    partner = lax.rem(col + 8, PIECES)
    send(None, turned.at[pl.ds(0, 4)], slab(col, 4), pair, at(dy=2))
    my_head = qi.at[4, pl.ds(pl.multiple_of(col * part, part), part)]
    for r in range(8):
        if r:
            send(row == 0, turned.at[4], my_head, head, (r, col))
        send(row == 0, turned.at[4], my_head, head2, (r, partner))
    keep4 = pltpu.make_async_copy(
        turned.at[pl.ds(0, 4)], slab(col, 4), local_sems.at[take("local")]
    )
    keep4.start()
    keep1 = pltpu.make_async_copy(turned.at[4], my_head, local_sems.at[take("local")])
    pl.when(row == 0)(lambda: keep1.start())

    for s in range(CHUNKS // 2):
        l_step(s)

    arrive(None, slab(partner, 4), pair)
    arrive(row != 0, my_head, head)
    arrive(None, qi.at[4, pl.ds(pl.multiple_of(partner * part, part), part)], head2)
    keep4.wait()
    pl.when(row == 0)(lambda: keep1.wait())

    def near(piece, dx):
        return 8 * (piece // 8) + 2 * lax.rem(x + dx, 4) + k

    right = take("recv", 2)
    left = take("recv", 2)
    far = take("recv", 2)
    core = take("recv", 8)
    both = (8 * 0 + 2 * x + k, 8 + 2 * x + k)
    for h in range(2):
        send(None, slab(both[h]), slab(both[h]), right + h, at(dx=1))
        send(None, slab(both[h]), slab(both[h]), left + h, at(dx=3))
    for h in range(2):
        send(None, slab(both[h]), slab(both[h]), core + h, at(dk=1))
    for s in range(CHUNKS // 2, CHUNKS):
        l_step(s)
    for h in (0, 1):
        from_left, from_right = near(both[h], 3), near(both[h], 1)
        arrive(None, slab(from_left), right + h)
        if h == 0:
            send(None, slab(from_left), slab(from_left), far, at(dx=1))
        send(None, slab(from_left), slab(from_left), core + 2 + h, at(dk=1))
        arrive(None, slab(from_right), left + h)
        if h == 1:
            send(None, slab(from_right), slab(from_right), far + 1, at(dx=3))
        send(None, slab(from_right), slab(from_right), core + 4 + h, at(dk=1))
    for h in (0, 1):
        opposite = near(both[h], 2)
        arrive(None, slab(opposite), far + h)
        send(None, slab(opposite), slab(opposite), core + 6 + h, at(dk=1))
    for n, dx in enumerate((0, 3, 1, 2)):
        for h in range(2):
            theirs = 8 * h + 2 * lax.rem(x + dx, 4) + lax.rem(k + 1, 2)
            arrive(None, slab(theirs), core + 2 * n + h)

    l_finish()
    q_start, q_step, q_finish = exchange(qi, qj)
    q_start()
    for s in range(CHUNKS):
        q_step(s)
    q_finish()
    for cond, body in open_sends:
        when(cond, body)
    assert used["send"] <= send_sems.shape[0], used
    assert used["recv"] <= recv_sems.shape[0], used
    assert used["local"] <= local_sems.shape[0], used


def gather(a, low, dinv):
    nb = dinv.shape[0]
    part = nb // PIECES
    anywhere = pl.BlockSpec(memory_space=pltpu.HBM)
    return pl.pallas_call(
        gather_kernel,
        out_shape=(
            jax.ShapeDtypeStruct((5, nb, nb), F32),
            jax.ShapeDtypeStruct((2, nb, nb), F32),
            jax.ShapeDtypeStruct((2, nb, nb), F32),
        ),
        in_specs=[anywhere, anywhere, pl.BlockSpec(memory_space=pltpu.VMEM)],
        out_specs=(anywhere, anywhere, anywhere),
        scratch_shapes=[
            pltpu.VMEM((4, part, 4, 128), F32),
            pltpu.VMEM((5, part, nb), F32),
            pltpu.VMEM((nb, nb), BF),
            pltpu.VMEM((nb, nb), BF),
            pltpu.SemaphoreType.DMA((160,)),
            pltpu.SemaphoreType.DMA((90,)),
            pltpu.SemaphoreType.DMA((10,)),
        ],
        compiler_params=pltpu.CompilerParams(
            collective_id=0, has_side_effects=True, vmem_limit_bytes=16 << 20
        ),
        name="gather",
    )(a, low, dinv)


def update_kernel(a, qi, li, lj, qj, r, dinv, o, yh, yl, ch, cl, sh, sl, cf, xh, xl):
    b = pl.program_id(0)
    row, col = lax.axis_index("row"), lax.axis_index("col")

    @pl.when(b == 0)
    def _():
        @pl.loop(0, 2)
        def _(c):
            rows = pl.ds(pl.multiple_of(c * 512, 512), 512)
            yh[rows, :512], yl[rows, :512] = split(lj[c])
            yh[rows, 512:], yl[rows, 512:] = split(qj[c])

        dh, dl = split(dinv[...])
        rh, rl = split(r[0])
        cf[...] = dot3(dh, dl, rh, rl, NN)
        ch[...], cl[...] = split(cf[...])
        sh[...], sl[...] = split(0.5 * (cf[...] + cf[...].T))

    xh[:, 512:], xl[:, 512:] = split(li[0])

    @pl.loop(0, 2)
    def _(m):
        rows = pl.ds(pl.multiple_of(m * 256, 256), 256)
        f = qi[0, rows, :] - dot3(xh[rows, 512:], xl[rows, 512:], sh[...], sl[...], NN)
        xh[rows, :512], xl[rows, :512] = split(f)

    @pl.loop(0, 4)
    def _(n):
        c, half = n // 2, lax.rem(n, 2)
        rows = pl.ds(pl.multiple_of(n * 256, 256), 256)
        cols = pl.ds(pl.multiple_of(half * 256, 256), 256)
        top = jnp.logical_and(row == 0, b == 0)
        side = jnp.logical_and(col == 0, c == 0)

        def put(values):
            for t in range(2):
                o[pl.ds(n * 2 + t, 512, stride=8), :] = values(t)

        @pl.when(jnp.logical_not(jnp.logical_or(top, side)))
        def _():
            acc = dot3(xh[...], xl[...], yh[rows, :], yl[rows, :], NT)
            put(
                lambda t: a[pl.ds(n * 2 + t, 512, stride=8), :]
                - acc[:, t * 128 : (t + 1) * 128]
            )

        @pl.when(jnp.logical_and(side, jnp.logical_not(top)))
        def _():
            fin = qi[0, :, cols] - dot3(
                xh[:, 512:], xl[:, 512:], ch[:, cols], cl[:, cols], NN
            )
            put(lambda t: fin[:, t * 128 : (t + 1) * 128])

        @pl.when(jnp.logical_and(top, jnp.logical_not(side)))
        def _():
            fin = qj[c, cols, :] - dot3(
                yh[rows, :512], yl[rows, :512], ch[...], cl[...], NN
            )
            fin = fin.T
            put(lambda t: fin[:, t * 128 : (t + 1) * 128])

        @pl.when(jnp.logical_and(top, side))
        def _():
            fin = cf[:, cols]
            put(lambda t: fin[:, t * 128 : (t + 1) * 128])


def update(a, qi, li, lj, qj, dinv):
    nb = dinv.shape[0]
    pairs = pl.BlockSpec((2, nb, nb), lambda b: (0, 0, 0))
    block = pl.BlockSpec((1, nb, nb), lambda b: (b, 0, 0))
    linear = pl.BlockSpec((8 * nb, 128), lambda b: (b, 0))
    return pl.pallas_call(
        update_kernel,
        grid=(4,),
        out_shape=jax.ShapeDtypeStruct(a.shape, F32),
        in_specs=[
            linear,
            block,
            block,
            pairs,
            pairs,
            pl.BlockSpec((1, nb, nb), lambda b: (4, 0, 0)),
            pl.BlockSpec((nb, nb), lambda b: (0, 0)),
        ],
        out_specs=linear,
        scratch_shapes=[pltpu.VMEM((2 * nb, 2 * nb), BF)] * 2
        + [pltpu.VMEM((nb, nb), BF)] * 4
        + [pltpu.VMEM((nb, nb), F32)]
        + [pltpu.VMEM((nb, 2 * nb), BF)] * 2,
        compiler_params=pltpu.CompilerParams(vmem_limit_bytes=56 << 20),
        name="update",
    )(a, qi, li, lj, qj, qi, dinv)


def body(stiffness, lower_panel, diag_inverse):
    shape = stiffness.shape
    tiles = stiffness.reshape(4, 512, 2, 4, 128)
    rows = stiffness.reshape(16384, 128)
    low = lower_panel[:, 0]
    qi, lj, qj = gather(tiles, low, diag_inverse)
    out = update(rows, qi, low, lj, qj, diag_inverse)
    return out.reshape(shape)


def solution(mesh):
    in_specs = (P(None, "row", None, None, "col", None), P(None, "row", None, None), P())
    out_specs = P(None, "row", None, None, "col", None)
    return jax.shard_map(body, mesh=mesh, in_specs=in_specs, out_specs=out_specs, check_vma=False)
```

```python
import functools

import jax
import jax.numpy as jnp
from jax import lax
from jax.experimental import pallas as pl
from jax.experimental.pallas import tpu as pltpu
from jax.sharding import PartitionSpec as P

F32, BF = jnp.float32, jnp.bfloat16
MESH = pl.DeviceIdType.MESH
NT = (((1,), (1,)), ((), ()))
NN = (((1,), (0,)), ((), ()))
PIECES = 16
CHUNKS = 8


def split(x):
    high = x.astype(BF)
    return high, (x - high.astype(F32)).astype(BF)


def dot3(ah, al, bh, bl, dims):
    dot = functools.partial(
        lax.dot_general, dimension_numbers=dims, preferred_element_type=F32
    )
    return dot(ah, bh) + dot(ah, bl) + dot(al, bh)


def gather_kernel(
    a, low, dinv, qi_out, lj_out, qj_out, raw, turned, dh, dl, qi, lj, qj, send_sems, recv_sems, local_sems
):
    row, col = lax.axis_index("row"), lax.axis_index("col")
    z, yl = row // 2, lax.rem(row, 2)
    yh, x, k = col // 8, lax.rem(col // 2, 4), lax.rem(col, 2)
    y = 2 * yh + yl
    nb = dinv.shape[0]
    part = nb // PIECES

    def at(dx=0, dy=0, dz=0, dk=0):
        nx, ny = lax.rem(x + dx + 4, 4), lax.rem(y + dy + 4, 4)
        nz, nk = lax.rem(z + dz + 4, 4), lax.rem(k + dk, 2)
        return (2 * nz + lax.rem(ny, 2), 8 * (ny // 2) + 2 * nx + nk)

    used = {"send": 0, "recv": 0, "local": 0}
    open_sends = []

    def take(kind, count=1):
        first = used[kind]
        used[kind] += count
        return first

    def when(cond, body):
        if cond is None:
            body()
        else:
            pl.when(cond)(body)

    def send(tag, cond, src, dst, recv, device):
        sem = take("send")

        def copy():
            return pltpu.make_async_remote_copy(
                src_ref=src,
                dst_ref=dst,
                send_sem=send_sems.at[sem],
                recv_sem=recv_sems.at[recv],
                device_id=device,
                device_id_type=MESH,
            )

        when(cond, lambda: copy().start())
        open_sends.append((cond, lambda: copy().wait_send()))

    def arrive(tag, cond, dst, recv):
        def body():
            pltpu.make_async_remote_copy(
                src_ref=dst,
                dst_ref=dst,
                send_sem=send_sems.at[0],
                recv_sem=recv_sems.at[recv],
                device_id=at(dk=1),
                device_id_type=MESH,
            ).wait_recv()

        when(cond, body)

    def keep(src, dst):
        return pltpu.make_async_copy(src, dst, local_sems.at[take("local")])

    barrier = pltpu.get_barrier_semaphore()

    def greet(cond, device):
        when(
            cond,
            lambda: pl.semaphore_signal(
                barrier, inc=1, device_id=device, device_id_type=MESH
            ),
        )

    neighbours = [at(dx=1), at(dx=3), at(dy=1), at(dy=3), at(dz=1), at(dz=3), at(dy=2), at(dk=1)]
    for device in neighbours:
        greet(None, device)
    greet(col != 0, (row, 0))
    greet(row != 0, (0, col))
    greet(None, (0, lax.rem(col + 8, PIECES)))
    expect = (
        len(neighbours)
        + jnp.where(col == 0, PIECES - 1, 0)
        + jnp.where(row == 0, 7 + 8, 0)
    )
    pl.semaphore_wait(barrier, expect)

    raw_recv = take("recv")
    for piece in range(1, PIECES):
        send(
            "S",
            col == 0,
            a.at[:, pl.ds(piece * part, part), 0],
            raw,
            raw_recv,
            (row, piece),
        )
    own_raw = keep(a.at[:, pl.ds(0, part), 0], raw)
    pl.when(col == 0)(lambda: own_raw.start())

    dz = lax.rem(z - x + 4, 4)
    size = nb // CHUNKS

    def exchange(tag, source, target):
        mine = jnp.logical_and(dz == 0, yl == k)
        cross = take("recv", 2 * CHUNKS)
        ring = take("recv", 2 * CHUNKS)
        own = [keep(source.at[2 * c + yh], target.at[c]) for c in range(2)]
        hops = (dz, lax.rem(4 - dz, 4))
        up = (at(dz=1), at(dz=3))
        relay = [take("send", CHUNKS) for c in range(2)]

        def rows(s):
            return pl.ds(pl.multiple_of(s * size, size), size)

        def start():
            @pl.when(mine)
            def _():
                for copy in own:
                    copy.start()

            for s in range(CHUNKS):
                for c, dy in ((0, 1), (1, 3)):
                    their = lax.rem(y + dy, 4) // 2
                    send(
                        tag,
                        mine,
                        source.at[2 * c + their, rows(s)],
                        target.at[c, rows(s)],
                        cross + c * CHUNKS + s,
                        at(dy=dy),
                    )
                    send(
                        tag,
                        mine,
                        source.at[2 * c + yh, rows(s)],
                        target.at[c, rows(s)],
                        ring + c * CHUNKS + s,
                        up[c],
                    )

        def onward(c, s):
            here = target.at[c, rows(s)]
            return pltpu.make_async_remote_copy(
                src_ref=here,
                dst_ref=here,
                send_sem=send_sems.at[relay[c] + s],
                recv_sem=recv_sems.at[ring + c * CHUNKS + s],
                device_id=up[c],
                device_id_type=MESH,
            )

        def step(t):
            for c in range(2):
                s = t - hops[c]
                live = jnp.logical_and(jnp.logical_not(mine), jnp.logical_and(s >= 0, s < CHUNKS))
                here = target.at[c, rows(s)]
                arrive(tag, jnp.logical_and(live, dz == 0), here, cross + c * CHUNKS + s)
                arrive(tag, jnp.logical_and(live, dz != 0), here, ring + c * CHUNKS + s)
                when_live(tag, jnp.logical_and(live, hops[c] != 3), lambda: onward(c, s).start())

        def finish():
            @pl.when(mine)
            def _():
                for copy in own:
                    copy.wait()

            for c in range(2):
                cond = jnp.logical_and(jnp.logical_not(mine), hops[c] != 3)

                def body():
                    @pl.loop(0, CHUNKS)
                    def _(s):
                        onward(c, s).wait_send()

                when_live(tag, cond, body)

        return start, step, finish

    def when_live(tag, cond, body):
        when(cond, body)

    l_start, l_step, l_finish = exchange("L", low, lj)
    q_start, q_step, q_finish = exchange("Q", qi, qj)
    STEPS = CHUNKS + 3
    l_start()

    dh[...], dl[...] = split(dinv[...])
    arrive("S", col != 0, raw, raw_recv)
    pl.when(col == 0)(lambda: own_raw.wait())

    for b in range(4):
        rows = jnp.concatenate([raw[b, :, t, :] for t in range(4)], axis=1)
        high, lo = split(rows)
        turned[b] = dot3(high, lo, dh[...], dl[...], NT)

    def slab(piece, count=5):
        return qi.at[pl.ds(0, count), pl.ds(pl.multiple_of(piece * part, part), part)]

    head = take("recv")
    head2 = take("recv")
    pair = take("recv")
    partner = lax.rem(col + 8, PIECES)
    send("Y", None, turned, slab(col, 4), pair, at(dy=2))
    my_head = qi.at[4, pl.ds(pl.multiple_of(col * part, part), part)]
    for r in range(8):
        if r:
            send("R", row == 0, turned.at[0], my_head, head, (r, col))
        send("R", row == 0, turned.at[0], my_head, head2, (r, partner))
    keep4 = keep(turned, slab(col, 4))
    keep4.start()
    keep1 = keep(turned.at[0], my_head)
    pl.when(row == 0)(lambda: keep1.start())

    for t in range(STEPS // 2):
        l_step(t)

    arrive("Y", None, slab(partner, 4), pair)
    arrive("R", row != 0, my_head, head)
    arrive("R", None, qi.at[4, pl.ds(pl.multiple_of(partner * part, part), part)], head2)
    keep4.wait()
    pl.when(row == 0)(lambda: keep1.wait())

    def near(piece, dx):
        return 8 * (piece // 8) + 2 * lax.rem(x + dx, 4) + k

    right = take("recv", 2)
    left = take("recv", 2)
    far = take("recv", 2)
    core = take("recv", 8)
    both = (2 * x + k, 8 + 2 * x + k)
    for h in range(2):
        send("X", None, slab(both[h]), slab(both[h]), right + h, at(dx=1))
        send("X", None, slab(both[h]), slab(both[h]), left + h, at(dx=3))
    for h in range(2):
        send("K", None, slab(both[h]), slab(both[h]), core + h, at(dk=1))
    for t in range(STEPS // 2, STEPS):
        l_step(t)
    for h in (0, 1):
        from_left, from_right = near(both[h], 3), near(both[h], 1)
        arrive("X", None, slab(from_left), right + h)
        if h == 0:
            send("X", None, slab(from_left), slab(from_left), far, at(dx=1))
        send("K", None, slab(from_left), slab(from_left), core + 2 + h, at(dk=1))
        arrive("X", None, slab(from_right), left + h)
        if h == 1:
            send("X", None, slab(from_right), slab(from_right), far + 1, at(dx=3))
        send("K", None, slab(from_right), slab(from_right), core + 4 + h, at(dk=1))
    for h in (0, 1):
        opposite = near(both[h], 2)
        arrive("X", None, slab(opposite), far + h)
        send("K", None, slab(opposite), slab(opposite), core + 6 + h, at(dk=1))
    for n, dx in enumerate((0, 3, 1, 2)):
        for h in range(2):
            theirs = 8 * h + 2 * lax.rem(x + dx, 4) + lax.rem(k + 1, 2)
            arrive("K", None, slab(theirs), core + 2 * n + h)

    l_finish()
    q_start()
    qi_save = keep(qi, qi_out)
    qi_save.start()
    lj_save = keep(lj, lj_out)
    lj_save.start()

    @pl.loop(0, STEPS)
    def _(t):
        q_step(t)

    q_finish()
    qj_save = keep(qj, qj_out)
    qj_save.start()
    for cond, body in open_sends:
        when(cond, body)
    qi_save.wait()
    lj_save.wait()
    qj_save.wait()
    assert used["send"] <= send_sems.shape[0], used
    assert used["recv"] <= recv_sems.shape[0], used
    assert used["local"] <= local_sems.shape[0], used


def gather(a, low, dinv):
    nb = dinv.shape[0]
    part = nb // PIECES
    anywhere = pl.BlockSpec(memory_space=pl.ANY)
    return pl.pallas_call(
        gather_kernel,
        out_shape=(
            jax.ShapeDtypeStruct((5, nb, nb), F32),
            jax.ShapeDtypeStruct((2, nb, nb), F32),
            jax.ShapeDtypeStruct((2, nb, nb), F32),
        ),
        in_specs=[anywhere, anywhere, pl.BlockSpec(memory_space=pltpu.VMEM)],
        out_specs=(anywhere, anywhere, anywhere),
        scratch_shapes=[
            pltpu.VMEM((4, part, 4, 128), F32),
            pltpu.VMEM((4, part, nb), F32),
            pltpu.VMEM((nb, nb), BF),
            pltpu.VMEM((nb, nb), BF),
            pltpu.VMEM((5, nb, nb), F32),
            pltpu.VMEM((2, nb, nb), F32),
            pltpu.VMEM((2, nb, nb), F32),
            pltpu.SemaphoreType.DMA((190,)),
            pltpu.SemaphoreType.DMA((90,)),
            pltpu.SemaphoreType.DMA((12,)),
        ],
        compiler_params=pltpu.CompilerParams(
            collective_id=0, has_side_effects=True, vmem_limit_bytes=60 << 20
        ),
        name="gather",
    )(a, low, dinv)


def update_kernel(a, qi, li, lj, qj, r, dinv, o, yh, yl, ch, cl, sh, sl, cf, xh, xl):
    b = pl.program_id(0)
    row, col = lax.axis_index("row"), lax.axis_index("col")

    @pl.when(b == 0)
    def _():
        @pl.loop(0, 2)
        def _(c):
            rows = pl.ds(pl.multiple_of(c * 512, 512), 512)
            yh[rows, :512], yl[rows, :512] = split(lj[c])
            yh[rows, 512:], yl[rows, 512:] = split(qj[c])

        dh, dl = split(dinv[...])
        rh, rl = split(r[0])
        cf[...] = dot3(dh, dl, rh, rl, NN)
        ch[...], cl[...] = split(cf[...])
        sh[...], sl[...] = split(0.5 * (cf[...] + cf[...].T))

    xh[:, 512:], xl[:, 512:] = split(li[0])

    @pl.loop(0, 2)
    def _(m):
        rows = pl.ds(pl.multiple_of(m * 256, 256), 256)
        f = qi[0, rows, :] - dot3(xh[rows, 512:], xl[rows, 512:], sh[...], sl[...], NN)
        xh[rows, :512], xl[rows, :512] = split(f)

    @pl.loop(0, 4)
    def _(n):
        c, half = n // 2, lax.rem(n, 2)
        rows = pl.ds(pl.multiple_of(n * 256, 256), 256)
        cols = pl.ds(pl.multiple_of(half * 256, 256), 256)
        top = jnp.logical_and(row == 0, b == 0)
        side = jnp.logical_and(col == 0, c == 0)

        def put(values):
            for t in range(2):
                o[pl.ds(n * 2 + t, 512, stride=8), :] = values(t)

        @pl.when(jnp.logical_not(jnp.logical_or(top, side)))
        def _():
            acc = dot3(xh[...], xl[...], yh[rows, :], yl[rows, :], NT)
            put(
                lambda t: a[pl.ds(n * 2 + t, 512, stride=8), :]
                - acc[:, t * 128 : (t + 1) * 128]
            )

        @pl.when(jnp.logical_and(side, jnp.logical_not(top)))
        def _():
            fin = qi[0, :, cols] - dot3(
                xh[:, 512:], xl[:, 512:], ch[:, cols], cl[:, cols], NN
            )
            put(lambda t: fin[:, t * 128 : (t + 1) * 128])

        @pl.when(jnp.logical_and(top, jnp.logical_not(side)))
        def _():
            fin = qj[c, cols, :] - dot3(
                yh[rows, :512], yl[rows, :512], ch[...], cl[...], NN
            )
            fin = fin.T
            put(lambda t: fin[:, t * 128 : (t + 1) * 128])

        @pl.when(jnp.logical_and(top, side))
        def _():
            fin = cf[:, cols]
            put(lambda t: fin[:, t * 128 : (t + 1) * 128])


def update(a, qi, li, lj, qj, dinv):
    nb = dinv.shape[0]
    pairs = pl.BlockSpec((2, nb, nb), lambda b: (0, 0, 0))
    block = pl.BlockSpec((1, nb, nb), lambda b: (b, 0, 0))
    linear = pl.BlockSpec((8 * nb, 128), lambda b: (b, 0))
    return pl.pallas_call(
        update_kernel,
        grid=(4,),
        out_shape=jax.ShapeDtypeStruct(a.shape, F32),
        in_specs=[
            linear,
            block,
            block,
            pairs,
            pairs,
            pl.BlockSpec((1, nb, nb), lambda b: (4, 0, 0)),
            pl.BlockSpec((nb, nb), lambda b: (0, 0)),
        ],
        out_specs=linear,
        scratch_shapes=[pltpu.VMEM((2 * nb, 2 * nb), BF)] * 2
        + [pltpu.VMEM((nb, nb), BF)] * 4
        + [pltpu.VMEM((nb, nb), F32)]
        + [pltpu.VMEM((nb, 2 * nb), BF)] * 2,
        compiler_params=pltpu.CompilerParams(vmem_limit_bytes=56 << 20),
        name="update",
    )(a, qi, li, lj, qj, qi, dinv)


def body(stiffness, lower_panel, diag_inverse):
    shape = stiffness.shape
    tiles = stiffness.reshape(4, 512, 2, 4, 128)
    rows = stiffness.reshape(16384, 128)
    low = lower_panel[:, 0]
    qi, lj, qj = gather(tiles, low, diag_inverse)
    out = update(rows, qi, low, lj, qj, diag_inverse)
    return out.reshape(shape)


def solution(mesh):
    in_specs = (P(None, "row", None, None, "col", None), P(None, "row", None, None), P())
    out_specs = P(None, "row", None, None, "col", None)
    return jax.shard_map(body, mesh=mesh, in_specs=in_specs, out_specs=out_specs, check_vma=False)
```

```python
import functools

import jax
import jax.numpy as jnp
from jax import lax
from jax.experimental import pallas as pl
from jax.experimental.pallas import tpu as pltpu
from jax.sharding import PartitionSpec as P

F32, BF = jnp.float32, jnp.bfloat16
MESH = pl.DeviceIdType.MESH
NT = (((1,), (1,)), ((), ()))
NN = (((1,), (0,)), ((), ()))
PIECES = 16
CHUNKS = 8


def split(x):
    high = x.astype(BF)
    return high, (x - high.astype(F32)).astype(BF)


def dot3(ah, al, bh, bl, dims):
    dot = functools.partial(
        lax.dot_general, dimension_numbers=dims, preferred_element_type=F32
    )
    return dot(ah, bh) + dot(ah, bl) + dot(al, bh)


def gather_kernel(
    a, low, dinv, qi_out, lj_out, qj_out, raw, turned, dh, dl, qi, lj, qj, send_sems, recv_sems, local_sems
):
    row, col = lax.axis_index("row"), lax.axis_index("col")
    z, yl = row // 2, lax.rem(row, 2)
    yh, x, k = col // 8, lax.rem(col // 2, 4), lax.rem(col, 2)
    y = 2 * yh + yl
    nb = dinv.shape[0]
    part = nb // PIECES

    def at(dx=0, dy=0, dz=0, dk=0):
        nx, ny = lax.rem(x + dx + 4, 4), lax.rem(y + dy + 4, 4)
        nz, nk = lax.rem(z + dz + 4, 4), lax.rem(k + dk, 2)
        return (2 * nz + lax.rem(ny, 2), 8 * (ny // 2) + 2 * nx + nk)

    used = {"send": 0, "recv": 0, "local": 0}
    open_sends = []

    def take(kind, count=1):
        first = used[kind]
        used[kind] += count
        return first

    def when(cond, body):
        if cond is None:
            body()
        else:
            pl.when(cond)(body)

    def send(tag, cond, src, dst, recv, device):
        sem = take("send")

        def copy():
            return pltpu.make_async_remote_copy(
                src_ref=src,
                dst_ref=dst,
                send_sem=send_sems.at[sem],
                recv_sem=recv_sems.at[recv],
                device_id=device,
                device_id_type=MESH,
            )

        when(cond, lambda: copy().start())
        open_sends.append((cond, lambda: copy().wait_send()))

    def arrive(tag, cond, dst, recv):
        def body():
            pltpu.make_async_remote_copy(
                src_ref=dst,
                dst_ref=dst,
                send_sem=send_sems.at[0],
                recv_sem=recv_sems.at[recv],
                device_id=at(dk=1),
                device_id_type=MESH,
            ).wait_recv()

        when(cond, body)

    def keep(src, dst):
        return pltpu.make_async_copy(src, dst, local_sems.at[take("local")])

    barrier = pltpu.get_barrier_semaphore()

    def greet(cond, device):
        when(
            cond,
            lambda: pl.semaphore_signal(
                barrier, inc=1, device_id=device, device_id_type=MESH
            ),
        )

    neighbours = [at(dx=1), at(dx=3), at(dy=1), at(dy=3), at(dz=1), at(dz=3), at(dy=2), at(dk=1)]
    for device in neighbours:
        greet(None, device)
    greet(col != 0, (row, 0))
    greet(row != 0, (0, col))
    greet(None, (0, lax.rem(col + 8, PIECES)))
    expect = (
        len(neighbours)
        + jnp.where(col == 0, PIECES - 1, 0)
        + jnp.where(row == 0, 7 + 8, 0)
    )
    pl.semaphore_wait(barrier, expect)

    def place(eighth, upper, count=1):
        return pl.ds(pl.multiple_of((2 * eighth + upper) * part, part), count * part)

    raw_recv = take("recv")
    for piece in range(1, PIECES):
        send(
            "S",
            col == 0,
            a.at[:, place(piece % 8, piece // 8), 0],
            raw,
            raw_recv,
            (row, piece),
        )
    own_raw = keep(a.at[:, place(0, 0), 0], raw)
    pl.when(col == 0)(lambda: own_raw.start())

    dz = lax.rem(z - x + 4, 4)
    mine = jnp.logical_and(dz == 0, yl == k)
    relays = jnp.logical_not(mine)
    lag = jnp.where(yl == k, 0, 1)
    hops = (dz, lax.rem(4 - dz, 4))
    up = (at(dz=1), at(dz=3))

    def exchange(tag, source, target, chunks, rows):
        cross = take("recv", 2 * chunks)
        ring = take("recv", 2 * chunks)
        relay = take("send", 2 * chunks)

        def start(s):
            for c, dy in ((0, 1), (1, 3)):
                their = lax.rem(y + dy, 4) // 2
                send(
                    tag,
                    mine,
                    source.at[2 * c + yh, rows(s)],
                    target.at[c, rows(s)],
                    ring + c * chunks + s,
                    up[c],
                )
                send(
                    tag,
                    mine,
                    source.at[2 * c + their, rows(s)],
                    target.at[c, rows(s)],
                    cross + c * chunks + s,
                    at(dy=dy),
                )

        def onward(c, s):
            here = target.at[c, rows(s)]
            return pltpu.make_async_remote_copy(
                src_ref=here,
                dst_ref=here,
                send_sem=send_sems.at[relay + c * chunks + s],
                recv_sem=recv_sems.at[ring + c * chunks + s],
                device_id=up[c],
                device_id_type=MESH,
            )

        def step(t, group=1):
            for c in range(2):
                first = t - hops[c] - lag
                live = jnp.logical_and(
                    relays, jnp.logical_and(first >= 0, first < chunks // group)
                )
                for e in range(group):
                    s = first * group + e
                    here = target.at[c, rows(s)]
                    arrive(tag, jnp.logical_and(live, dz == 0), here, cross + c * chunks + s)
                    arrive(tag, jnp.logical_and(live, dz != 0), here, ring + c * chunks + s)
                    tagged(tag, jnp.logical_and(live, hops[c] != 3), lambda: onward(c, s).start())

        def finish():
            for c in range(2):

                def body():
                    @pl.loop(0, chunks)
                    def _(s):
                        onward(c, s).wait_send()

                tagged(tag, jnp.logical_and(relays, hops[c] != 3), body)

        return start, step, finish

    def tagged(tag, cond, body):
        when(cond, body)

    def own_blocks(source, target):
        return [keep(source.at[2 * c + yh], target.at[c]) for c in range(2)]

    size = nb // CHUNKS
    l_start, l_step, l_finish = exchange(
        "L", low, lj, CHUNKS, lambda s: pl.ds(pl.multiple_of(s * size, size), size)
    )
    l_own = own_blocks(low, lj)

    def slice_rows(s):
        group, other, e = s // 4, lax.rem(s // 2, 2), lax.rem(s, 2)
        ends = jnp.logical_or(group == 0, group == 3)
        upper = jnp.where(ends, e, group - 1)
        dx = jnp.where(group == 0, 0, jnp.where(group == 3, 2, 3 - 2 * e))
        return place(2 * lax.rem(x + dx, 4) + lax.rem(k + other, 2), upper)

    q_start, q_step, q_finish = exchange("Q", qi, qj, PIECES, slice_rows)
    q_own = own_blocks(qi, qj)

    @pl.when(mine)
    def _():
        for copy in l_own:
            copy.start()

    for s in range(CHUNKS):
        l_start(s)
    dh[...], dl[...] = split(dinv[...])
    for t in range(6):
        l_step(t)
    arrive("S", col != 0, raw, raw_recv)
    pl.when(col == 0)(lambda: own_raw.wait())

    rows = jnp.concatenate(
        [
            jnp.concatenate([raw[b, :, t, :] for t in range(4)], axis=1)
            for b in range(4)
        ],
        axis=0,
    )
    high, lo = split(rows)
    turned[...] = dot3(high, lo, dh[...], dl[...], NT).reshape(turned.shape)

    eighth = lax.rem(col, 8)
    across = lax.rem(col + 8, PIECES)

    def slab(here, count=1):
        return qi.at[pl.ds(0, 4), place(*here, count)]

    def head(here, count=1):
        return qi.at[4, place(*here, count)]

    def near(dx, dk=0):
        return 2 * lax.rem(x + dx, 4) + lax.rem(k + dk, 2)

    own, partner = (eighth, yh), (eighth, 1 - yh)
    pair = take("recv")
    send("Y", None, turned, slab(own), pair, at(dy=2))
    head_own, head_partner = take("recv"), take("recv")
    for r in range(8):
        if r:
            send("R", row == 0, turned.at[0], head(own), head_own, (r, col))
        send("R", row == 0, turned.at[0], head(own), head_partner, (r, across))
    keep_slab = keep(turned, slab(own))
    keep_slab.start()
    keep_head = keep(turned.at[0], head(own))
    pl.when(row == 0)(lambda: keep_head.start())
    for t in range(6, 9):
        l_step(t)
    keep_slab.wait()
    arrive("Y", None, slab(partner), pair)

    right, left, far = take("recv", 2), take("recv", 2), take("recv", 2)
    core_own, core_side, core_far = take("recv"), take("recv", 4), take("recv", 2)
    h_right, h_left, h_far, h_core = (
        take("recv"), take("recv"), take("recv"), take("recv", 4)
    )

    def pass_on(event):
        for s in (2 * event, 2 * event + 1):
            q_start(s)
        q_step(event, 2)

    for h in range(2):
        for target, dx in ((right, 1), (left, 3)):
            send("X", None, slab((eighth, h)), slab((eighth, h)), target + h, at(dx=dx))
    send("K", None, slab((eighth, 0), 2), slab((eighth, 0), 2), core_own, at(dk=1))
    pass_on(0)
    arrive("K", None, slab((near(0, 1), 0), 2), core_own)
    pass_on(1)
    for t in range(9, 12):
        l_step(t)
    for h in range(2):
        for n, (source, dx) in enumerate(((right, 3), (left, 1))):
            here = slab((near(dx), h))
            arrive("X", None, here, source + h)
            if n == h:
                send("X", None, here, here, far + h, at(dx=4 - dx))
            send("K", None, here, here, core_side + 2 * h + n, at(dk=1))
        pass_on(2 + 2 * h)
        if h == 1:
            pl.when(row == 0)(lambda: keep_head.wait())
            arrive("R", row != 0, head(own), head_own)
            arrive("R", None, head(partner), head_partner)
            mid = (eighth, 0)
            send("R", None, head(mid, 2), head(mid, 2), h_right, at(dx=1))
            send("R", None, head(mid, 2), head(mid, 2), h_left, at(dx=3))
            send("R", None, head(mid, 2), head(mid, 2), h_core, at(dk=1))
        for n, dx in enumerate((3, 1)):
            arrive("K", None, slab((near(dx, 1), h)), core_side + 2 * h + n)
        pass_on(3 + 2 * h)
    for h in range(2):
        here = slab((near(2), h))
        arrive("X", None, here, far + h)
        send("K", None, here, here, core_far + h, at(dk=1))
    pass_on(6)
    for n, (source, dx) in enumerate(((h_right, 3), (h_left, 1))):
        here = head((near(dx), 0), 2)
        arrive("R", None, here, source)
        if n == 0:
            send("R", None, here, here, h_far, at(dx=1))
        send("R", None, here, here, h_core + 1 + n, at(dk=1))
    for h in range(2):
        arrive("K", None, slab((near(2, 1), h)), core_far + h)
    pass_on(7)

    @pl.when(mine)
    def _():
        for copy in q_own:
            copy.start()

    q_step(8, 2)
    here = head((near(2), 0), 2)
    arrive("R", None, here, h_far)
    send("R", None, here, here, h_core + 3, at(dk=1))
    q_step(9, 2)
    for n, dx in enumerate((0, 3, 1, 2)):
        arrive("R", None, head((near(dx, 1), 0), 2), h_core + n)
    qi_save = keep(qi, qi_out)
    qi_save.start()
    q_step(10, 2)

    @pl.when(mine)
    def _():
        for copy in l_own + q_own:
            copy.wait()

    lj_save = keep(lj, lj_out)
    lj_save.start()
    q_step(11, 2)
    qj_save = keep(qj, qj_out)
    qj_save.start()
    l_finish()
    q_finish()
    for cond, body in open_sends:
        when(cond, body)
    qi_save.wait()
    lj_save.wait()
    qj_save.wait()
    assert used["send"] <= send_sems.shape[0], used
    assert used["recv"] <= recv_sems.shape[0], used
    assert used["local"] <= local_sems.shape[0], used


def gather(a, low, dinv):
    nb = dinv.shape[0]
    part = nb // PIECES
    anywhere = pl.BlockSpec(memory_space=pl.ANY)
    return pl.pallas_call(
        gather_kernel,
        out_shape=(
            jax.ShapeDtypeStruct((5, nb, nb), F32),
            jax.ShapeDtypeStruct((2, nb, nb), F32),
            jax.ShapeDtypeStruct((2, nb, nb), F32),
        ),
        in_specs=[anywhere, anywhere, pl.BlockSpec(memory_space=pltpu.VMEM)],
        out_specs=(anywhere, anywhere, anywhere),
        scratch_shapes=[
            pltpu.VMEM((4, part, 4, 128), F32),
            pltpu.VMEM((4, part, nb), F32),
            pltpu.VMEM((nb, nb), BF),
            pltpu.VMEM((nb, nb), BF),
            pltpu.VMEM((5, nb, nb), F32),
            pltpu.VMEM((2, nb, nb), F32),
            pltpu.VMEM((2, nb, nb), F32),
            pltpu.SemaphoreType.DMA((250,)),
            pltpu.SemaphoreType.DMA((140,)),
            pltpu.SemaphoreType.DMA((16,)),
        ],
        compiler_params=pltpu.CompilerParams(
            collective_id=0, has_side_effects=True, vmem_limit_bytes=60 << 20
        ),
        name="gather",
    )(a, low, dinv)


def update_kernel(a, qi, li, lj, qj, r, dinv, o, ys, xs, ch, cl, cf):
    b = pl.program_id(0)
    row, col = lax.axis_index("row"), lax.axis_index("col")
    nb = 512

    def halves(to, rows, at, values, low_twice):
        high, lo = split(values)
        for n in range(3):
            is_low = n == (1 if low_twice else 2)
            to[rows, pl.ds(2 * n * nb + at, nb)] = lo if is_low else high

    @pl.when(b == 0)
    def _():
        dh, dl = split(dinv[...])
        rh, rl = split(r[0])
        cf[...] = dot3(dh, dl, rh, rl, NN)
        ch[...], cl[...] = split(cf[...])
        sh, sl = split(0.5 * (cf[...] + cf[...].T))

        for c in range(2):
            rows = pl.ds(c * nb, nb)
            halves(ys, rows, 0, lj[c], True)
            g = qj[c] - dot3(ys[rows, :nb], ys[rows, pl.ds(2 * nb, nb)], sh, sl, NN)
            halves(ys, rows, nb, g, True)

    halves(xs, slice(None), 0, qi[0], False)
    halves(xs, slice(None), nb, li[0], False)

    @pl.loop(0, 2)
    def _(c):
        rows = pl.ds(pl.multiple_of(c * nb, nb), nb)
        top = jnp.logical_and(row == 0, b == 0)
        side = jnp.logical_and(col == 0, c == 0)

        def put(values):
            for t in range(4):
                o[pl.ds(c * 4 + t, nb, stride=8), :] = values(t)

        @pl.when(jnp.logical_not(jnp.logical_or(top, side)))
        def _():
            acc = lax.dot_general(xs[...], ys[rows, :], NT, preferred_element_type=F32)
            put(
                lambda t: a[pl.ds(c * 4 + t, nb, stride=8), :]
                - acc[:, t * 128 : (t + 1) * 128]
            )

        @pl.when(jnp.logical_and(side, jnp.logical_not(top)))
        def _():
            fin = qi[0] - dot3(
                xs[:, pl.ds(nb, nb)], xs[:, pl.ds(5 * nb, nb)], ch[...], cl[...], NN
            )
            put(lambda t: fin[:, t * 128 : (t + 1) * 128])

        @pl.when(jnp.logical_and(top, jnp.logical_not(side)))
        def _():
            fin = qj[c] - dot3(
                ys[rows, :nb], ys[rows, pl.ds(2 * nb, nb)], ch[...], cl[...], NN
            )
            fin = fin.T
            put(lambda t: fin[:, t * 128 : (t + 1) * 128])

        @pl.when(jnp.logical_and(top, side))
        def _():
            put(lambda t: cf[:, t * 128 : (t + 1) * 128])


def update(a, qi, li, lj, qj, dinv):
    nb = dinv.shape[0]
    pairs = pl.BlockSpec((2, nb, nb), lambda b: (0, 0, 0))
    block = pl.BlockSpec((1, nb, nb), lambda b: (b, 0, 0))
    linear = pl.BlockSpec((8 * nb, 128), lambda b: (b, 0))
    return pl.pallas_call(
        update_kernel,
        grid=(4,),
        out_shape=jax.ShapeDtypeStruct(a.shape, F32),
        in_specs=[
            linear,
            block,
            block,
            pairs,
            pairs,
            pl.BlockSpec((1, nb, nb), lambda b: (4, 0, 0)),
            pl.BlockSpec((nb, nb), lambda b: (0, 0)),
        ],
        out_specs=linear,
        scratch_shapes=[
            pltpu.VMEM((2 * nb, 6 * nb), BF),
            pltpu.VMEM((nb, 6 * nb), BF),
            pltpu.VMEM((nb, nb), BF),
            pltpu.VMEM((nb, nb), BF),
            pltpu.VMEM((nb, nb), F32),
        ],
        compiler_params=pltpu.CompilerParams(vmem_limit_bytes=56 << 20),
        name="update",
    )(a, qi, li, lj, qj, qi, dinv)


def body(stiffness, lower_panel, diag_inverse):
    shape = stiffness.shape
    tiles = stiffness.reshape(4, 512, 2, 4, 128)
    rows = stiffness.reshape(16384, 128)
    low = lower_panel[:, 0]
    qi, lj, qj = gather(tiles, low, diag_inverse)
    out = update(rows, qi, low, lj, qj, diag_inverse)
    return out.reshape(shape)


def solution(mesh):
    in_specs = (P(None, "row", None, None, "col", None), P(None, "row", None, None), P())
    out_specs = P(None, "row", None, None, "col", None)
    return jax.shard_map(body, mesh=mesh, in_specs=in_specs, out_specs=out_specs, check_vma=False)
```

```python
import functools

import jax
import jax.numpy as jnp
from jax import lax
from jax.experimental import pallas as pl
from jax.experimental.pallas import tpu as pltpu
from jax.sharding import PartitionSpec as P

F32, BF = jnp.float32, jnp.bfloat16
MESH = pl.DeviceIdType.MESH
NT = (((1,), (1,)), ((), ()))
NN = (((1,), (0,)), ((), ()))
PIECES = 16
CHUNKS = 8


def split(x):
    high = x.astype(BF)
    return high, (x - high.astype(F32)).astype(BF)


def dot3(ah, al, bh, bl, dims):
    dot = functools.partial(
        lax.dot_general, dimension_numbers=dims, preferred_element_type=F32
    )
    return dot(ah, bh) + dot(ah, bl) + dot(al, bh)


def gather_kernel(
    a, low, dinv, xh_out, xl_out, yh_out, yl_out, c_out,
    raw, turned, dh, dl, li, qi, lj, qj, xh, xl, yh, yl, cf, sh, sl, send_sems, recv_sems, local_sems,
):
    row, col = lax.axis_index("row"), lax.axis_index("col")
    z, ylo = row // 2, lax.rem(row, 2)
    yhi, x, k = col // 8, lax.rem(col // 2, 4), lax.rem(col, 2)
    y = 2 * yhi + ylo
    nb = dinv.shape[0]
    part = nb // PIECES

    def at(dx=0, dy=0, dz=0, dk=0):
        nx, ny = lax.rem(x + dx + 4, 4), lax.rem(y + dy + 4, 4)
        nz, nk = lax.rem(z + dz + 4, 4), lax.rem(k + dk, 2)
        return (2 * nz + lax.rem(ny, 2), 8 * (ny // 2) + 2 * nx + nk)

    used = {"send": 0, "recv": 0, "local": 0}
    open_sends = []

    def take(kind, count=1):
        first = used[kind]
        used[kind] += count
        return first

    def when(cond, body):
        if cond is None:
            body()
        else:
            pl.when(cond)(body)

    def tagged(tag, cond, body):
        when(cond, body)

    def send(tag, cond, src, dst, recv, device):
        sem = take("send")

        def copy():
            return pltpu.make_async_remote_copy(
                src_ref=src,
                dst_ref=dst,
                send_sem=send_sems.at[sem],
                recv_sem=recv_sems.at[recv],
                device_id=device,
                device_id_type=MESH,
            )

        when(cond, lambda: copy().start())
        open_sends.append((cond, lambda: copy().wait_send()))

    def arrive(tag, cond, dst, recv):
        def body():
            pltpu.make_async_remote_copy(
                src_ref=dst,
                dst_ref=dst,
                send_sem=send_sems.at[0],
                recv_sem=recv_sems.at[recv],
                device_id=at(dk=1),
                device_id_type=MESH,
            ).wait_recv()

        when(cond, body)

    def keep(src, dst):
        return pltpu.make_async_copy(src, dst, local_sems.at[take("local")])

    load_low = keep(low, li)
    load_low.start()
    barrier = pltpu.get_barrier_semaphore()

    def greet(cond, device):
        when(
            cond,
            lambda: pl.semaphore_signal(
                barrier, inc=1, device_id=device, device_id_type=MESH
            ),
        )

    neighbours = [at(dx=1), at(dx=3), at(dy=1), at(dy=3), at(dz=1), at(dz=3), at(dy=2), at(dk=1)]
    greet(col != 0, (row, 0))
    for device in neighbours:
        greet(None, device)
    greet(row != 0, (0, col))
    expect = (
        len(neighbours)
        + jnp.where(col == 0, PIECES - 1, 0)
        + jnp.where(row == 0, 7, 0)
    )
    pl.semaphore_wait(barrier, expect)

    def place(eighth, upper, count=1):
        return pl.ds(pl.multiple_of((2 * eighth + upper) * part, part), count * part)

    raw_recv = take("recv")
    for piece in range(1, PIECES):
        send(
            "S",
            col == 0,
            a.at[:, place(piece % 8, piece // 8), 0],
            raw,
            raw_recv,
            (row, piece),
        )
    own_raw = keep(a.at[:, place(0, 0), 0], raw)
    pl.when(col == 0)(lambda: own_raw.start())

    dz = lax.rem(z - x + 4, 4)
    mine = jnp.logical_and(dz == 0, ylo == k)
    relays = jnp.logical_not(mine)
    lag = jnp.where(ylo == k, 0, 1)
    hops = (dz, lax.rem(4 - dz, 4))
    up = (at(dz=1), at(dz=3))
    order = tuple(
        jnp.where(ylo == k, yhi, lax.rem(y + dy, 4) // 2) for dy in (3, 1)
    )

    def exchange(tag, source, target, chunks, rows):
        cross = take("recv", 2 * chunks)
        ring = take("recv", 2 * chunks)
        relay = take("send", 2 * chunks)

        def start(s):
            for c, dy in ((0, 1), (1, 3)):
                their = lax.rem(y + dy, 4) // 2
                here = rows(s, yhi)
                send(tag, mine, source.at[2 * c + yhi, here], target.at[c, here], ring + c * chunks + s, up[c])
                send(tag, mine, source.at[2 * c + their, here], target.at[c, here], cross + c * chunks + s, at(dy=dy))

        def onward(c, s):
            here = target.at[c, rows(s, order[c])]
            return pltpu.make_async_remote_copy(
                src_ref=here,
                dst_ref=here,
                send_sem=send_sems.at[relay + c * chunks + s],
                recv_sem=recv_sems.at[ring + c * chunks + s],
                device_id=up[c],
                device_id_type=MESH,
            )

        def step(t, group=1):
            for c in range(2):
                first = t - hops[c] - lag
                live = jnp.logical_and(
                    relays, jnp.logical_and(first >= 0, first < chunks // group)
                )
                for e in range(group):
                    s = first * group + e
                    here = target.at[c, rows(s, order[c])]
                    arrive(tag, jnp.logical_and(live, dz == 0), here, cross + c * chunks + s)
                    arrive(tag, jnp.logical_and(live, dz != 0), here, ring + c * chunks + s)
                    tagged(tag, jnp.logical_and(live, hops[c] != 3), lambda: onward(c, s).start())

        def finish():
            for c in range(2):

                def body():
                    @pl.loop(0, chunks)
                    def _(s):
                        onward(c, s).wait_send()

                tagged(tag, jnp.logical_and(relays, hops[c] != 3), body)

        return start, step, finish

    def own_blocks(source, target):
        return [keep(source.at[2 * c + yhi], target.at[c]) for c in range(2)]

    size = nb // CHUNKS
    l_start, l_step, l_finish = exchange(
        "L", low, lj, CHUNKS, lambda s, half: pl.ds(pl.multiple_of(s * size, size), size)
    )
    l_own = own_blocks(low, lj)

    def slice_rows(s, half):
        group, other, e = s // 4, lax.rem(s // 2, 2), lax.rem(s, 2)
        ends = jnp.logical_or(group == 0, group == 3)
        second = jnp.where(ends, e, group - 1)
        upper = jnp.where(second == 0, half, 1 - half)
        dx = jnp.where(group == 0, 0, jnp.where(group == 3, 2, 3 - 2 * e))
        return place(2 * lax.rem(x + dx, 4) + lax.rem(k + other, 2), upper)

    q_start, q_step, q_finish = exchange("Q", qi, qj, PIECES, slice_rows)
    q_own = own_blocks(qi, qj)

    def spread(source, target, half, count=8):
        size = nb // count

        @pl.loop(0, count)
        def _(n):
            rows = pl.ds(pl.multiple_of(n * size, size), size)
            cols = pl.ds(half * nb, nb)
            target[0][rows, cols], target[1][rows, cols] = split(source[rows, :])

    @pl.when(mine)
    def _():
        for copy in l_own:
            copy.start()

    for s in range(CHUNKS):
        l_start(s)
    dh[...], dl[...] = split(dinv[...])
    l_step(0)
    load_low.wait()
    for b in range(4):
        spread(li.at[b], (xh.at[b], xl.at[b]), 1)
        l_step(1 + b)
    arrive("S", col != 0, raw, raw_recv)
    pl.when(col == 0)(lambda: own_raw.wait())

    rows = jnp.concatenate(
        [
            jnp.concatenate([raw[b, :, t, :] for t in range(4)], axis=1)
            for b in range(4)
        ],
        axis=0,
    )
    high, lo = split(rows)
    turned[...] = dot3(high, lo, dh[...], dl[...], NT).reshape(turned.shape)

    def near(dx, dk=0):
        return 2 * lax.rem(x + dx, 4) + lax.rem(k + dk, 2)

    halves = (yhi, 1 - yhi)

    def slab(eighth, upper):
        return qi.at[pl.ds(0, 4), place(eighth, upper)]

    def head(eighth, upper, count=1):
        return qi.at[4, place(eighth, upper, count)]

    def into_halves(eighth, upper):
        here = place(eighth, upper)

        @pl.loop(0, 4)
        def _(b):
            xh[b, here, pl.ds(0, nb)], xl[b, here, pl.ds(0, nb)] = split(qi[b, here, :])

    right, left, far, core = take("recv", 2), take("recv", 2), take("recv", 2), take("recv", 8)
    pair, head_own, head_partner = take("recv"), take("recv"), take("recv")
    h_right, h_left, h_far, h_core = take("recv"), take("recv"), take("recv"), take("recv", 4)

    def side(n, src):
        here = slab(near(0), halves[n])
        send("X", None, src, here, right + n, at(dx=1))
        send("X", None, src, here, left + n, at(dx=3))
        send("K", None, src, here, core + n, at(dk=1))

    def pass_on(event):
        for s in (2 * event, 2 * event + 1):
            q_start(s)
        q_step(event, 2)

    send("Y", None, turned, slab(near(0), yhi), pair, at(dy=2))
    side(0, turned)
    my_head = head(near(0), yhi)
    for r in range(1, 8):
        send("R", row == 0, turned.at[0], my_head, head_own, (r, col))
    keep_slab = keep(turned, slab(near(0), yhi))
    keep_slab.start()
    keep_head = keep(turned.at[0], my_head)
    pl.when(row == 0)(lambda: keep_head.start())
    keep_slab.wait()
    q_start(0)
    arrive("Y", None, slab(near(0), 1 - yhi), pair)
    side(1, slab(near(0), 1 - yhi))
    q_start(1)
    pl.when(row == 0)(lambda: keep_head.wait())
    arrive("R", row != 0, my_head, head_own)
    send("R", None, my_head, my_head, head_partner, at(dy=2))
    q_step(0, 2)
    l_step(5)
    for n in range(2):
        arrive("K", None, slab(near(0, 1), halves[n]), core + n)
    pass_on(1)
    l_step(6)
    for n in range(2):
        into_halves(near(0), n)
        into_halves(near(0, 1), n)
    for h in range(2):
        for n, (source, dx) in enumerate(((right, 3), (left, 1))):
            here = slab(near(dx), halves[h])
            arrive("X", None, here, source + h)
            if n == h:
                send("X", None, here, here, far + h, at(dx=4 - dx))
            send("K", None, here, here, core + 2 + 2 * h + n, at(dk=1))
        pass_on(2 + 2 * h)
        if h == 0:
            arrive("R", None, head(near(0), 1 - yhi), head_partner)
            mid = head(near(0), 0, 2)
            send("R", None, mid, mid, h_right, at(dx=1))
            send("R", None, mid, mid, h_left, at(dx=3))
            send("R", None, mid, mid, h_core, at(dk=1))
        else:
            for n, (source, dx) in enumerate(((h_right, 3), (h_left, 1))):
                here = head(near(dx), 0, 2)
                arrive("R", None, here, source)
                if n == 0:
                    send("R", None, here, here, h_far, at(dx=1))
                send("R", None, here, here, h_core + 1 + n, at(dk=1))
        l_step(7 + 2 * h)
        for n, dx in enumerate((3, 1)):
            arrive("K", None, slab(near(dx, 1), halves[h]), core + 2 + 2 * h + n)
        pass_on(3 + 2 * h)
        l_step(8 + 2 * h)
        for dx in (3, 1):
            into_halves(near(dx), halves[h])
            into_halves(near(dx, 1), halves[h])
    for h in range(2):
        here = slab(near(2), halves[h])
        arrive("X", None, here, far + h)
        send("K", None, here, here, core + 6 + h, at(dk=1))
    pass_on(6)
    here = head(near(2), 0, 2)
    arrive("R", None, here, h_far)
    send("R", None, here, here, h_core + 3, at(dk=1))
    l_step(11)
    for h in range(2):
        arrive("K", None, slab(near(2, 1), halves[h]), core + 6 + h)
    pass_on(7)

    @pl.when(mine)
    def _():
        for copy in q_own:
            copy.start()

    saves = []

    def save(pairs):
        for src, dst in pairs:
            one = keep(src, dst)
            one.start()
            saves.append(one)

    for n in range(2):
        into_halves(near(2), n)
        into_halves(near(2, 1), n)
    save([(xh, xh_out), (xl, xl_out)])

    @pl.when(mine)
    def _():
        for copy in l_own:
            copy.wait()

    for c in range(2):
        spread(lj.at[c], (yh.at[c], yl.at[c]), 0)
    q_step(8, 2)
    for n, dx in enumerate((0, 3, 1, 2)):
        arrive("R", None, head(near(dx, 1), 0, 2), h_core + n)

    rh, rl = split(qi[4])
    cf[...] = dot3(dh[...], dl[...], rh, rl, NN)
    sh[...], sl[...] = split(0.5 * (cf[...] + cf[...].T))
    save([(cf, c_out)])
    q_step(9, 2)
    l_finish()
    lj[0] = dot3(yh[0, :, :nb], yl[0, :, :nb], sh[...], sl[...], NN)
    q_step(10, 2)
    lj[1] = dot3(yh[1, :, :nb], yl[1, :, :nb], sh[...], sl[...], NN)
    q_step(11, 2)

    @pl.when(mine)
    def _():
        for copy in q_own:
            copy.wait()

    for c in range(2):

        @pl.loop(0, 8)
        def _(n):
            here = pl.ds(pl.multiple_of(n * (nb // 8), nb // 8), nb // 8)
            cols = pl.ds(nb, nb)
            yh[c, here, cols], yl[c, here, cols] = split(qj[c, here, :] - lj[c, here, :])

        save([(yh.at[c], yh_out.at[c]), (yl.at[c], yl_out.at[c])])
    q_finish()
    for cond, body in open_sends:
        when(cond, body)
    for one in saves:
        one.wait()
    assert used["send"] <= send_sems.shape[0], used
    assert used["recv"] <= recv_sems.shape[0], used
    assert used["local"] <= local_sems.shape[0], used


def gather(a, low, dinv):
    nb = dinv.shape[0]
    part = nb // PIECES
    anywhere = pl.BlockSpec(memory_space=pl.ANY)
    return pl.pallas_call(
        gather_kernel,
        out_shape=(
            jax.ShapeDtypeStruct((4, nb, 2 * nb), BF),
            jax.ShapeDtypeStruct((4, nb, 2 * nb), BF),
            jax.ShapeDtypeStruct((2, nb, 2 * nb), BF),
            jax.ShapeDtypeStruct((2, nb, 2 * nb), BF),
            jax.ShapeDtypeStruct((nb, nb), F32),
        ),
        in_specs=[anywhere, anywhere, pl.BlockSpec(memory_space=pltpu.VMEM)],
        out_specs=(anywhere,) * 5,
        scratch_shapes=[
            pltpu.VMEM((4, part, 4, 128), F32),
            pltpu.VMEM((4, part, nb), F32),
            pltpu.VMEM((nb, nb), BF),
            pltpu.VMEM((nb, nb), BF),
            pltpu.VMEM((4, nb, nb), F32),
            pltpu.VMEM((5, nb, nb), F32),
            pltpu.VMEM((2, nb, nb), F32),
            pltpu.VMEM((2, nb, nb), F32),
            pltpu.VMEM((4, nb, 2 * nb), BF),
            pltpu.VMEM((4, nb, 2 * nb), BF),
            pltpu.VMEM((2, nb, 2 * nb), BF),
            pltpu.VMEM((2, nb, 2 * nb), BF),
            pltpu.VMEM((nb, nb), F32),
            pltpu.VMEM((nb, nb), BF),
            pltpu.VMEM((nb, nb), BF),
            pltpu.SemaphoreType.DMA((280,)),
            pltpu.SemaphoreType.DMA((140,)),
            pltpu.SemaphoreType.DMA((32,)),
        ],
        compiler_params=pltpu.CompilerParams(
            collective_id=0, has_side_effects=True, vmem_limit_bytes=60 << 20
        ),
        name="gather",
    )(a, low, dinv)


def update_kernel(a, xh, xl, yh, yl, cf, o, ch, cl, sh, sl):
    b = pl.program_id(0)
    row, col = lax.axis_index("row"), lax.axis_index("col")
    nb = cf.shape[0]
    edge = jnp.logical_or(row == 0, col == 0)

    @pl.when(jnp.logical_and(b == 0, edge))
    def _():
        ch[...], cl[...] = split(cf[...])
        sh[...], sl[...] = split(0.5 * (cf[...] - cf[...].T))

    dot = functools.partial(
        lax.dot_general, dimension_numbers=NT, preferred_element_type=F32
    )

    @pl.loop(0, 2)
    def _(c):
        top = jnp.logical_and(row == 0, b == 0)
        side = jnp.logical_and(col == 0, c == 0)

        def put(values):
            for t in range(4):
                o[pl.ds(c * 4 + t, nb, stride=8), :] = values(t)

        @pl.when(jnp.logical_not(jnp.logical_or(top, side)))
        def _():
            acc = dot(xh[0], yh[c]) + dot(xh[0], yl[c]) + dot(xl[0], yh[c])
            put(
                lambda t: a[pl.ds(c * 4 + t, nb, stride=8), :]
                - acc[:, t * 128 : (t + 1) * 128]
            )

        @pl.when(jnp.logical_and(side, jnp.logical_not(top)))
        def _():
            fin = dot3(xh[0, :, nb:], xl[0, :, nb:], ch[...], cl[...], NN)
            fin = (xh[0, :, :nb].astype(F32) + xl[0, :, :nb].astype(F32)) - fin
            put(lambda t: fin[:, t * 128 : (t + 1) * 128])

        @pl.when(jnp.logical_and(top, jnp.logical_not(side)))
        def _():
            fin = dot3(yh[c, :, :nb], yl[c, :, :nb], sh[...], sl[...], NN)
            fin = (yh[c, :, nb:].astype(F32) + yl[c, :, nb:].astype(F32)) - fin
            fin = fin.T
            put(lambda t: fin[:, t * 128 : (t + 1) * 128])

        @pl.when(jnp.logical_and(top, side))
        def _():
            put(lambda t: cf[:, t * 128 : (t + 1) * 128])


def update(a, xh, xl, yh, yl, cf):
    nb = cf.shape[0]
    pairs = pl.BlockSpec((2, nb, 2 * nb), lambda b: (0, 0, 0))
    block = pl.BlockSpec((1, nb, 2 * nb), lambda b: (b, 0, 0))
    linear = pl.BlockSpec((8 * nb, 128), lambda b: (b, 0))
    return pl.pallas_call(
        update_kernel,
        grid=(4,),
        out_shape=jax.ShapeDtypeStruct(a.shape, F32),
        in_specs=[linear, block, block, pairs, pairs, pl.BlockSpec((nb, nb), lambda b: (0, 0))],
        out_specs=linear,
        scratch_shapes=[pltpu.VMEM((nb, nb), BF)] * 4,
        compiler_params=pltpu.CompilerParams(vmem_limit_bytes=56 << 20),
        name="update",
    )(a, xh, xl, yh, yl, cf)


def body(stiffness, lower_panel, diag_inverse):
    tiles = stiffness.reshape(4, 512, 2, 4, 128)
    rows = stiffness.reshape(16384, 128)
    out = update(rows, *gather(tiles, lower_panel[:, 0], diag_inverse))
    return out.reshape(stiffness.shape)


def solution(mesh):
    in_specs = (P(None, "row", None, None, "col", None), P(None, "row", None, None), P())
    out_specs = P(None, "row", None, None, "col", None)
    return jax.shard_map(body, mesh=mesh, in_specs=in_specs, out_specs=out_specs, check_vma=False)
```

```python
import functools

import jax
import jax.numpy as jnp
from jax import lax
from jax.experimental import pallas as pl
from jax.experimental.pallas import tpu as pltpu
from jax.sharding import PartitionSpec as P

F32, BF = jnp.float32, jnp.bfloat16
MESH = pl.DeviceIdType.MESH
NT = (((1,), (1,)), ((), ()))
NN = (((1,), (0,)), ((), ()))
PIECES = 16
CHUNKS = 8


def split(x):
    high = x.astype(BF)
    return high, (x - high.astype(F32)).astype(BF)


def dot3(ah, al, bh, bl, dims):
    dot = functools.partial(
        lax.dot_general, dimension_numbers=dims, preferred_element_type=F32
    )
    return dot(ah, bh) + dot(ah, bl) + dot(al, bh)


def gather_kernel(
    a, low, dinv, xh_out, xl_out, yh_out, yl_out, c_out,
    raw, turned, dh, dl, li, qi, lj, qj, xh, xl, yh, yl, cf, sh, sl, send_sems, recv_sems, local_sems,
):
    row, col = lax.axis_index("row"), lax.axis_index("col")
    z, ylo = row // 2, lax.rem(row, 2)
    yhi, x, k = col // 8, lax.rem(col // 2, 4), lax.rem(col, 2)
    y = 2 * yhi + ylo
    nb = dinv.shape[0]
    part = nb // PIECES

    def at(dx=0, dy=0, dz=0, dk=0):
        nx, ny = lax.rem(x + dx + 4, 4), lax.rem(y + dy + 4, 4)
        nz, nk = lax.rem(z + dz + 4, 4), lax.rem(k + dk, 2)
        return (2 * nz + lax.rem(ny, 2), 8 * (ny // 2) + 2 * nx + nk)

    used = {"send": 0, "recv": 0, "local": 0}
    open_sends = []

    def take(kind, count=1):
        first = used[kind]
        used[kind] += count
        return first

    def when(cond, body):
        if cond is None:
            body()
        else:
            pl.when(cond)(body)

    def tagged(tag, cond, body):
        when(cond, body)

    def send(tag, cond, src, dst, recv, device):
        sem = take("send")

        def copy():
            return pltpu.make_async_remote_copy(
                src_ref=src,
                dst_ref=dst,
                send_sem=send_sems.at[sem],
                recv_sem=recv_sems.at[recv],
                device_id=device,
                device_id_type=MESH,
            )

        when(cond, lambda: copy().start())
        open_sends.append((cond, lambda: copy().wait_send()))

    def arrive(tag, cond, dst, recv):
        def body():
            pltpu.make_async_remote_copy(
                src_ref=dst,
                dst_ref=dst,
                send_sem=send_sems.at[0],
                recv_sem=recv_sems.at[recv],
                device_id=at(dk=1),
                device_id_type=MESH,
            ).wait_recv()

        when(cond, body)

    def keep(src, dst):
        return pltpu.make_async_copy(src, dst, local_sems.at[take("local")])

    load_low = keep(low, li)
    load_low.start()
    barrier = pltpu.get_barrier_semaphore()

    def greet(cond, device):
        when(
            cond,
            lambda: pl.semaphore_signal(
                barrier, inc=1, device_id=device, device_id_type=MESH
            ),
        )

    neighbours = [at(dx=1), at(dx=3), at(dy=1), at(dy=3), at(dz=1), at(dz=3), at(dy=2), at(dk=1)]
    greet(col != 0, (row, 0))
    for device in neighbours:
        greet(None, device)
    greet(row != 0, (0, col))
    expect = (
        len(neighbours)
        + jnp.where(col == 0, PIECES - 1, 0)
        + jnp.where(row == 0, 7, 0)
    )
    pl.semaphore_wait(barrier, expect)

    def place(eighth, upper, count=1):
        return pl.ds(pl.multiple_of((2 * eighth + upper) * part, part), count * part)

    raw_recv = take("recv")
    for piece in range(1, PIECES):
        send(
            "S",
            col == 0,
            a.at[:, place(piece % 8, piece // 8), 0],
            raw,
            raw_recv,
            (row, piece),
        )
    own_raw = keep(a.at[:, place(0, 0), 0], raw)
    pl.when(col == 0)(lambda: own_raw.start())

    dz = lax.rem(z - x + 4, 4)
    chain = ylo == k
    mine = jnp.logical_and(dz == 0, chain)
    relays = jnp.logical_and(dz != 0, chain)
    hops = tuple(jnp.where(h == 3, 1, h) for h in (dz, lax.rem(4 - dz, 4)))
    passes = (dz == 1, dz == 3)
    up = (at(dz=1), at(dz=3))
    beside = at(dy=jnp.where(ylo == 0, 1, 3))

    def exchange(tag, source, target, chunks, rows):
        cross = take("recv", 2 * chunks)
        ring = take("recv", 2 * chunks)
        to_ring = take("send", 2 * chunks)
        to_cross = take("send", 2 * chunks)
        to_back = take("send", 2 * chunks)

        def move(src, here, sends, recvs, n, device):
            return pltpu.make_async_remote_copy(
                src_ref=src,
                dst_ref=here,
                send_sem=send_sems.at[sends + n],
                recv_sem=recv_sems.at[recvs + n],
                device_id=device,
                device_id_type=MESH,
            )

        def both_ways(c, s, src, here):
            n = c * chunks + s
            return (
                move(src, here, to_ring, ring, n, up[c]),
                move(src, here, to_cross, cross, n, beside),
            )

        def start(s):
            @pl.when(mine)
            def _():
                for c in range(2):
                    here = rows(s)
                    src, dst = source.at[2 * c + yhi, here], target.at[c, here]
                    for one in both_ways(c, s, src, dst):
                        one.start()
                    move(src, dst, to_back, ring, c * chunks + s, up[1 - c]).start()

        def step(t, group=1):
            for c in range(2):
                first = t - hops[c]
                live = jnp.logical_and(
                    relays, jnp.logical_and(first >= 0, first < chunks // group)
                )
                for e in range(group):
                    s = first * group + e
                    here = target.at[c, rows(s)]

                    @pl.when(live)
                    def _():
                        arrive(tag, None, here, ring + c * chunks + s)
                        onward, over = both_ways(c, s, here, here)
                        pl.when(passes[c])(lambda: onward.start())
                        over.start()

        def take_over():
            @pl.when(jnp.logical_not(chain))
            def _():
                @pl.loop(0, chunks)
                def _(s):
                    for c in range(2):
                        arrive(tag, None, target.at[c, rows(s)], cross + c * chunks + s)

        def finish():
            @pl.when(chain)
            def _():
                @pl.loop(0, chunks)
                def _(s):
                    for c in range(2):
                        here = target.at[c, rows(s)]
                        onward, over = both_ways(c, s, here, here)
                        n = c * chunks + s
                        pl.when(jnp.logical_or(mine, passes[c]))(lambda: onward.wait_send())
                        over.wait_send()
                        pl.when(mine)(
                            lambda: move(here, here, to_back, ring, n, up[1 - c]).wait_send()
                        )

        return start, step, take_over, finish

    def own_blocks(source, target):
        return [keep(source.at[2 * c + yhi], target.at[c]) for c in range(2)]

    size = nb // CHUNKS
    l_start, l_step, l_take_over, l_finish = exchange(
        "L", low, lj, CHUNKS, lambda s: pl.ds(pl.multiple_of(s * size, size), size)
    )
    l_own = own_blocks(low, lj)

    def slice_rows(s):
        group, other, e = s // 4, lax.rem(s // 2, 2), lax.rem(s, 2)
        ends = jnp.logical_or(group == 0, group == 3)
        second = jnp.where(ends, e, group - 1)
        upper = jnp.where(second == 0, yhi, 1 - yhi)
        dx = jnp.where(group == 0, 0, jnp.where(group == 3, 2, 3 - 2 * e))
        return place(2 * lax.rem(x + dx, 4) + lax.rem(k + other, 2), upper)

    q_start, q_step, q_take_over, q_finish = exchange("Q", qi, qj, PIECES, slice_rows)
    q_own = own_blocks(qi, qj)

    def spread(source, target, half, count=8):
        size = nb // count

        @pl.loop(0, count)
        def _(n):
            rows = pl.ds(pl.multiple_of(n * size, size), size)
            cols = pl.ds(half * nb, nb)
            target[0][rows, cols], target[1][rows, cols] = split(source[rows, :])

    @pl.when(mine)
    def _():
        for copy in l_own:
            copy.start()

    for s in range(CHUNKS):
        l_start(s)
    dh[...], dl[...] = split(dinv[...])
    l_step(0)
    load_low.wait()
    for b in range(4):
        spread(li.at[b], (xh.at[b], xl.at[b]), 1)
        l_step(1 + b)
    l_step(5)
    arrive("S", col != 0, raw, raw_recv)
    pl.when(col == 0)(lambda: own_raw.wait())

    rows = jnp.concatenate(
        [
            jnp.concatenate([raw[b, :, t, :] for t in range(4)], axis=1)
            for b in range(4)
        ],
        axis=0,
    )
    high, lo = split(rows)
    turned[...] = dot3(high, lo, dh[...], dl[...], NT).reshape(turned.shape)

    def near(dx, dk=0):
        return 2 * lax.rem(x + dx, 4) + lax.rem(k + dk, 2)

    halves = (yhi, 1 - yhi)

    def slab(eighth, upper):
        return qi.at[pl.ds(0, 4), place(eighth, upper)]

    def head(eighth, upper, count=1):
        return qi.at[4, place(eighth, upper, count)]

    def into_halves(eighth, upper):
        here = place(eighth, upper)

        @pl.loop(0, 4)
        def _(b):
            xh[b, here, pl.ds(0, nb)], xl[b, here, pl.ds(0, nb)] = split(qi[b, here, :])

    right, left, far, core = take("recv", 2), take("recv", 2), take("recv", 2), take("recv", 8)
    pair, head_own, head_partner = take("recv"), take("recv"), take("recv")
    h_right, h_left, h_far, h_core = take("recv"), take("recv"), take("recv"), take("recv", 4)

    def side(n, src):
        here = slab(near(0), halves[n])
        send("X", None, src, here, right + n, at(dx=1))
        send("X", None, src, here, left + n, at(dx=3))
        send("K", None, src, here, core + n, at(dk=1))

    def pass_on(event):
        for s in (2 * event, 2 * event + 1):
            q_start(s)
        q_step(event, 2)

    send("Y", None, turned, slab(near(0), yhi), pair, at(dy=2))
    side(0, turned)
    my_head = head(near(0), yhi)
    for r in range(1, 8):
        send("R", row == 0, turned.at[0], my_head, head_own, (r, col))
    keep_slab = keep(turned, slab(near(0), yhi))
    keep_slab.start()
    keep_head = keep(turned.at[0], my_head)
    pl.when(row == 0)(lambda: keep_head.start())
    l_step(6)
    keep_slab.wait()
    q_start(0)
    l_step(7)
    arrive("Y", None, slab(near(0), 1 - yhi), pair)
    side(1, slab(near(0), 1 - yhi))
    q_start(1)
    pl.when(row == 0)(lambda: keep_head.wait())
    arrive("R", row != 0, my_head, head_own)
    send("R", None, my_head, my_head, head_partner, at(dy=2))
    q_step(0, 2)
    l_step(8)
    for n in range(2):
        arrive("K", None, slab(near(0, 1), halves[n]), core + n)
    pass_on(1)
    l_step(9)
    for n in range(2):
        into_halves(near(0), n)
        into_halves(near(0, 1), n)
    for h in range(2):
        for n, (source, dx) in enumerate(((right, 3), (left, 1))):
            here = slab(near(dx), halves[h])
            arrive("X", None, here, source + h)
            if n == h:
                send("X", None, here, here, far + h, at(dx=4 - dx))
            send("K", None, here, here, core + 2 + 2 * h + n, at(dk=1))
        pass_on(2 + 2 * h)
        if h == 0:
            arrive("R", None, head(near(0), 1 - yhi), head_partner)
            mid = head(near(0), 0, 2)
            send("R", None, mid, mid, h_right, at(dx=1))
            send("R", None, mid, mid, h_left, at(dx=3))
            send("R", None, mid, mid, h_core, at(dk=1))
        else:
            for n, (source, dx) in enumerate(((h_right, 3), (h_left, 1))):
                here = head(near(dx), 0, 2)
                arrive("R", None, here, source)
                if n == 0:
                    send("R", None, here, here, h_far, at(dx=1))
                send("R", None, here, here, h_core + 1 + n, at(dk=1))
        for n, dx in enumerate((3, 1)):
            arrive("K", None, slab(near(dx, 1), halves[h]), core + 2 + 2 * h + n)
        pass_on(3 + 2 * h)
        if h == 0:

            @pl.when(mine)
            def _():
                for copy in l_own:
                    copy.wait()

            l_take_over()
            for c in range(2):
                spread(lj.at[c], (yh.at[c], yl.at[c]), 0)
        for dx in (3, 1):
            into_halves(near(dx), halves[h])
            into_halves(near(dx, 1), halves[h])
    for h in range(2):
        here = slab(near(2), halves[h])
        arrive("X", None, here, far + h)
        send("K", None, here, here, core + 6 + h, at(dk=1))
    pass_on(6)
    here = head(near(2), 0, 2)
    arrive("R", None, here, h_far)
    send("R", None, here, here, h_core + 3, at(dk=1))
    for h in range(2):
        arrive("K", None, slab(near(2, 1), halves[h]), core + 6 + h)
    pass_on(7)

    @pl.when(mine)
    def _():
        for copy in q_own:
            copy.start()

    saves = []

    def save(pairs):
        for src, dst in pairs:
            one = keep(src, dst)
            one.start()
            saves.append(one)

    q_step(8, 2)
    for n in range(2):
        into_halves(near(2), n)
        into_halves(near(2, 1), n)
    save([(xh, xh_out), (xl, xl_out)])
    q_step(9, 2)
    for n, dx in enumerate((0, 3, 1, 2)):
        arrive("R", None, head(near(dx, 1), 0, 2), h_core + n)

    rh, rl = split(qi[4])
    cf[...] = dot3(dh[...], dl[...], rh, rl, NN)
    sh[...], sl[...] = split(0.5 * (cf[...] + cf[...].T))
    save([(cf, c_out)])
    l_finish()
    for c in range(2):
        lj[c] = dot3(yh[c, :, :nb], yl[c, :, :nb], sh[...], sl[...], NN)
    q_take_over()

    @pl.when(mine)
    def _():
        for copy in q_own:
            copy.wait()

    for c in range(2):

        @pl.loop(0, 8)
        def _(n):
            here = pl.ds(pl.multiple_of(n * (nb // 8), nb // 8), nb // 8)
            cols = pl.ds(nb, nb)
            yh[c, here, cols], yl[c, here, cols] = split(qj[c, here, :] - lj[c, here, :])

        save([(yh.at[c], yh_out.at[c]), (yl.at[c], yl_out.at[c])])
    q_finish()
    for cond, body in open_sends:
        when(cond, body)
    for one in saves:
        one.wait()
    assert used["send"] <= send_sems.shape[0], used
    assert used["recv"] <= recv_sems.shape[0], used
    assert used["local"] <= local_sems.shape[0], used


def gather(a, low, dinv):
    nb = dinv.shape[0]
    part = nb // PIECES
    anywhere = pl.BlockSpec(memory_space=pl.ANY)
    return pl.pallas_call(
        gather_kernel,
        out_shape=(
            jax.ShapeDtypeStruct((4, nb, 2 * nb), BF),
            jax.ShapeDtypeStruct((4, nb, 2 * nb), BF),
            jax.ShapeDtypeStruct((2, nb, 2 * nb), BF),
            jax.ShapeDtypeStruct((2, nb, 2 * nb), BF),
            jax.ShapeDtypeStruct((nb, nb), F32),
        ),
        in_specs=[anywhere, anywhere, pl.BlockSpec(memory_space=pltpu.VMEM)],
        out_specs=(anywhere,) * 5,
        scratch_shapes=[
            pltpu.VMEM((4, part, 4, 128), F32),
            pltpu.VMEM((4, part, nb), F32),
            pltpu.VMEM((nb, nb), BF),
            pltpu.VMEM((nb, nb), BF),
            pltpu.VMEM((4, nb, nb), F32),
            pltpu.VMEM((5, nb, nb), F32),
            pltpu.VMEM((2, nb, nb), F32),
            pltpu.VMEM((2, nb, nb), F32),
            pltpu.VMEM((4, nb, 2 * nb), BF),
            pltpu.VMEM((4, nb, 2 * nb), BF),
            pltpu.VMEM((2, nb, 2 * nb), BF),
            pltpu.VMEM((2, nb, 2 * nb), BF),
            pltpu.VMEM((nb, nb), F32),
            pltpu.VMEM((nb, nb), BF),
            pltpu.VMEM((nb, nb), BF),
            pltpu.SemaphoreType.DMA((300,)),
            pltpu.SemaphoreType.DMA((140,)),
            pltpu.SemaphoreType.DMA((32,)),
        ],
        compiler_params=pltpu.CompilerParams(
            collective_id=0, has_side_effects=True, vmem_limit_bytes=60 << 20
        ),
        name="gather",
    )(a, low, dinv)


def update_kernel(a, xh, xl, yh, yl, cf, o, ch, cl, sh, sl):
    b = pl.program_id(0)
    row, col = lax.axis_index("row"), lax.axis_index("col")
    nb = cf.shape[0]
    edge = jnp.logical_or(row == 0, col == 0)

    @pl.when(jnp.logical_and(b == 0, edge))
    def _():
        ch[...], cl[...] = split(cf[...])
        sh[...], sl[...] = split(0.5 * (cf[...] - cf[...].T))

    dot = functools.partial(
        lax.dot_general, dimension_numbers=NT, preferred_element_type=F32
    )

    @pl.loop(0, 2)
    def _(c):
        top = jnp.logical_and(row == 0, b == 0)
        side = jnp.logical_and(col == 0, c == 0)

        def put(values):
            for t in range(4):
                o[pl.ds(c * 4 + t, nb, stride=8), :] = values(t)

        @pl.when(jnp.logical_not(jnp.logical_or(top, side)))
        def _():
            acc = dot(xh[0], yh[c]) + dot(xh[0], yl[c]) + dot(xl[0], yh[c])
            put(
                lambda t: a[pl.ds(c * 4 + t, nb, stride=8), :]
                - acc[:, t * 128 : (t + 1) * 128]
            )

        @pl.when(jnp.logical_and(side, jnp.logical_not(top)))
        def _():
            fin = dot3(xh[0, :, nb:], xl[0, :, nb:], ch[...], cl[...], NN)
            fin = (xh[0, :, :nb].astype(F32) + xl[0, :, :nb].astype(F32)) - fin
            put(lambda t: fin[:, t * 128 : (t + 1) * 128])

        @pl.when(jnp.logical_and(top, jnp.logical_not(side)))
        def _():
            fin = dot3(yh[c, :, :nb], yl[c, :, :nb], sh[...], sl[...], NN)
            fin = (yh[c, :, nb:].astype(F32) + yl[c, :, nb:].astype(F32)) - fin
            fin = fin.T
            put(lambda t: fin[:, t * 128 : (t + 1) * 128])

        @pl.when(jnp.logical_and(top, side))
        def _():
            put(lambda t: cf[:, t * 128 : (t + 1) * 128])


def update(a, xh, xl, yh, yl, cf):
    nb = cf.shape[0]
    pairs = pl.BlockSpec((2, nb, 2 * nb), lambda b: (0, 0, 0))
    block = pl.BlockSpec((1, nb, 2 * nb), lambda b: (b, 0, 0))
    linear = pl.BlockSpec((8 * nb, 128), lambda b: (b, 0))
    return pl.pallas_call(
        update_kernel,
        grid=(4,),
        out_shape=jax.ShapeDtypeStruct(a.shape, F32),
        in_specs=[linear, block, block, pairs, pairs, pl.BlockSpec((nb, nb), lambda b: (0, 0))],
        out_specs=linear,
        scratch_shapes=[pltpu.VMEM((nb, nb), BF)] * 4,
        compiler_params=pltpu.CompilerParams(vmem_limit_bytes=56 << 20),
        name="update",
    )(a, xh, xl, yh, yl, cf)


def body(stiffness, lower_panel, diag_inverse):
    tiles = stiffness.reshape(4, 512, 2, 4, 128)
    rows = stiffness.reshape(16384, 128)
    out = update(rows, *gather(tiles, lower_panel[:, 0], diag_inverse))
    return out.reshape(stiffness.shape)


def solution(mesh):
    in_specs = (P(None, "row", None, None, "col", None), P(None, "row", None, None), P())
    out_specs = P(None, "row", None, None, "col", None)
    return jax.shard_map(body, mesh=mesh, in_specs=in_specs, out_specs=out_specs, check_vma=False)
```

```python
import functools

import jax
import jax.numpy as jnp
from jax import lax
from jax.experimental import pallas as pl
from jax.experimental.pallas import tpu as pltpu
from jax.sharding import PartitionSpec as P

F32, BF = jnp.float32, jnp.bfloat16
MESH = pl.DeviceIdType.MESH
NT = (((1,), (1,)), ((), ()))
NN = (((1,), (0,)), ((), ()))
PIECES = 16
CHUNKS = 8


def split(x):
    high = x.astype(BF)
    return high, (x - high.astype(F32)).astype(BF)


def dot3(ah, al, bh, bl, dims):
    dot = functools.partial(
        lax.dot_general, dimension_numbers=dims, preferred_element_type=F32
    )
    return dot(ah, bh) + dot(ah, bl) + dot(al, bh)


def gather_kernel(
    a, blocks, low, dinv, a_out, lih_out, lil_out, gh_out, gl_out,
    raw, turned, dh, dl, li, qi, lj, qj, blk, qh, ql, lih, lil, ljh, ljl, gh, gl, cf, sh, sl,
    send_sems, recv_sems, local_sems,
):
    row, col = lax.axis_index("row"), lax.axis_index("col")
    z, ylo = row // 2, lax.rem(row, 2)
    yhi, x, k = col // 8, lax.rem(col // 2, 4), lax.rem(col, 2)
    y = 2 * yhi + ylo
    nb = dinv.shape[0]
    part = nb // PIECES

    def at(dx=0, dy=0, dz=0, dk=0):
        nx, ny = lax.rem(x + dx + 4, 4), lax.rem(y + dy + 4, 4)
        nz, nk = lax.rem(z + dz + 4, 4), lax.rem(k + dk, 2)
        return (2 * nz + lax.rem(ny, 2), 8 * (ny // 2) + 2 * nx + nk)

    used = {"send": 0, "recv": 0, "local": 0}
    open_sends = []

    def take(kind, count=1):
        first = used[kind]
        used[kind] += count
        return first

    def when(cond, body):
        if cond is None:
            body()
        else:
            pl.when(cond)(body)

    def tagged(tag, cond, body):
        when(cond, body)

    def send(tag, cond, src, dst, recv, device):
        sem = take("send")

        def copy():
            return pltpu.make_async_remote_copy(
                src_ref=src,
                dst_ref=dst,
                send_sem=send_sems.at[sem],
                recv_sem=recv_sems.at[recv],
                device_id=device,
                device_id_type=MESH,
            )

        when(cond, lambda: copy().start())
        open_sends.append((cond, lambda: copy().wait_send()))

    def arrive(tag, cond, dst, recv):
        def body():
            pltpu.make_async_remote_copy(
                src_ref=dst,
                dst_ref=dst,
                send_sem=send_sems.at[0],
                recv_sem=recv_sems.at[recv],
                device_id=at(dk=1),
                device_id_type=MESH,
            ).wait_recv()

        when(cond, body)

    def keep(src, dst):
        return pltpu.make_async_copy(src, dst, local_sems.at[take("local")])

    load_low = keep(low, li)
    load_low.start()
    load_blocks = keep(blocks, blk)
    load_blocks.start()
    barrier = pltpu.get_barrier_semaphore()

    def greet(cond, device):
        when(
            cond,
            lambda: pl.semaphore_signal(
                barrier, inc=1, device_id=device, device_id_type=MESH
            ),
        )

    neighbours = [at(dx=1), at(dx=3), at(dy=1), at(dy=3), at(dz=1), at(dz=3), at(dy=2), at(dk=1)]
    greet(col != 0, (row, 0))
    for device in neighbours:
        greet(None, device)
    greet(row != 0, (0, col))
    expect = (
        len(neighbours)
        + jnp.where(col == 0, PIECES - 1, 0)
        + jnp.where(row == 0, 7, 0)
    )
    pl.semaphore_wait(barrier, expect)

    def place(eighth, upper, count=1):
        return pl.ds(pl.multiple_of((2 * eighth + upper) * part, part), count * part)

    raw_recv = take("recv")
    for piece in (12, 10, 13, 11, 4, 2, 5, 3, 14, 8, 15, 9, 6, 1, 7):
        send(
            "S",
            col == 0,
            a.at[:, place(piece % 8, piece // 8), 0],
            raw,
            raw_recv,
            (row, piece),
        )
    own_raw = keep(a.at[:, place(0, 0), 0], raw)
    pl.when(col == 0)(lambda: own_raw.start())

    dz = lax.rem(z - x + 4, 4)
    chain = ylo == k
    mine = jnp.logical_and(dz == 0, chain)
    relays = jnp.logical_and(dz != 0, chain)
    hops = tuple(jnp.where(h == 3, 1, h) for h in (dz, lax.rem(4 - dz, 4)))
    passes = (dz == 1, dz == 3)
    up = (at(dz=1), at(dz=3))
    beside = at(dy=jnp.where(ylo == 0, 1, 3))

    def exchange(tag, source, target, chunks, rows):
        cross = take("recv", 2 * chunks)
        ring = take("recv", 2 * chunks)
        to_ring = take("send", 2 * chunks)
        to_cross = take("send", 2 * chunks)
        to_back = take("send", 2 * chunks)

        def move(src, here, sends, recvs, n, device):
            return pltpu.make_async_remote_copy(
                src_ref=src,
                dst_ref=here,
                send_sem=send_sems.at[sends + n],
                recv_sem=recv_sems.at[recvs + n],
                device_id=device,
                device_id_type=MESH,
            )

        def both_ways(c, s, src, here):
            n = c * chunks + s
            return (
                move(src, here, to_ring, ring, n, up[c]),
                move(src, here, to_cross, cross, n, beside),
            )

        def start(s):
            @pl.when(mine)
            def _():
                for c in range(2):
                    here = rows(s)
                    src, dst = source.at[2 * c + yhi, here], target.at[c, here]
                    for one in both_ways(c, s, src, dst):
                        one.start()
                    move(src, dst, to_back, ring, c * chunks + s, up[1 - c]).start()

        def step(t, group=1):
            for c in range(2):
                first = t - hops[c]
                live = jnp.logical_and(
                    relays, jnp.logical_and(first >= 0, first < chunks // group)
                )
                for e in range(group):
                    s = first * group + e
                    here = target.at[c, rows(s)]

                    @pl.when(live)
                    def _():
                        arrive(tag, None, here, ring + c * chunks + s)
                        onward, over = both_ways(c, s, here, here)
                        pl.when(passes[c])(lambda: onward.start())
                        over.start()

        def take_over():
            @pl.when(jnp.logical_not(chain))
            def _():
                @pl.loop(0, chunks)
                def _(s):
                    for c in range(2):
                        arrive(tag, None, target.at[c, rows(s)], cross + c * chunks + s)

        def finish():
            @pl.when(chain)
            def _():
                @pl.loop(0, chunks)
                def _(s):
                    for c in range(2):
                        here = target.at[c, rows(s)]
                        onward, over = both_ways(c, s, here, here)
                        n = c * chunks + s
                        pl.when(jnp.logical_or(mine, passes[c]))(lambda: onward.wait_send())
                        over.wait_send()
                        pl.when(mine)(
                            lambda: move(here, here, to_back, ring, n, up[1 - c]).wait_send()
                        )

        return start, step, take_over, finish

    def own_blocks(source, target):
        return [keep(source.at[2 * c + yhi], target.at[c]) for c in range(2)]

    size = nb // CHUNKS
    l_start, l_step, l_take_over, l_finish = exchange(
        "L", low, lj, CHUNKS, lambda s: pl.ds(pl.multiple_of(s * size, size), size)
    )
    l_own = own_blocks(low, lj)

    def slice_rows(s):
        group, other, e = s // 4, lax.rem(s // 2, 2), lax.rem(s, 2)
        ends = jnp.logical_or(group == 0, group == 3)
        second = jnp.where(ends, e, group - 1)
        upper = jnp.where(second == 0, yhi, 1 - yhi)
        dx = jnp.where(group == 0, 0, jnp.where(group == 3, 2, 3 - 2 * e))
        return place(2 * lax.rem(x + dx, 4) + lax.rem(k + other, 2), upper)

    q_start, q_step, q_take_over, q_finish = exchange("Q", qi, qj, PIECES, slice_rows)
    q_own = own_blocks(qi, qj)

    def spread(source, high, low_part, count=8):
        size = nb // count

        @pl.loop(0, count)
        def _(n):
            rows = pl.ds(pl.multiple_of(n * size, size), size)
            high[rows, :], low_part[rows, :] = split(source[rows, :])

    @pl.when(mine)
    def _():
        for copy in l_own:
            copy.start()

    for s in range(CHUNKS):
        l_start(s)
    dh[...], dl[...] = split(dinv[...])
    l_step(0)
    load_low.wait()
    for b in range(4):
        spread(li.at[b], lih.at[b], lil.at[b])
        l_step(1 + b)
    l_step(5)
    arrive("S", col != 0, raw, raw_recv)
    pl.when(col == 0)(lambda: own_raw.wait())

    rows = jnp.concatenate(
        [
            jnp.concatenate([raw[b, :, t, :] for t in range(4)], axis=1)
            for b in range(4)
        ],
        axis=0,
    )
    high, lo = split(rows)
    turned[...] = dot3(high, lo, dh[...], dl[...], NT).reshape(turned.shape)

    def near(dx, dk=0):
        return 2 * lax.rem(x + dx, 4) + lax.rem(k + dk, 2)

    halves = (yhi, 1 - yhi)

    def slab(eighth, upper):
        return qi.at[pl.ds(0, 4), place(eighth, upper)]

    def head(eighth, upper, count=1):
        return qi.at[4, place(eighth, upper, count)]

    def into_halves(eighth, upper):
        here = place(eighth, upper)

        @pl.loop(0, 4)
        def _(b):
            qh[b, here, :], ql[b, here, :] = split(qi[b, here, :])

    right, left, far, core = take("recv", 2), take("recv", 2), take("recv", 2), take("recv", 8)
    pair, head_own, head_partner = take("recv"), take("recv"), take("recv")
    h_right, h_left, h_far, h_core = take("recv"), take("recv"), take("recv"), take("recv", 4)

    def side(n, src):
        here = slab(near(0), halves[n])
        send("X", None, src, here, right + n, at(dx=1))
        send("X", None, src, here, left + n, at(dx=3))
        send("K", None, src, here, core + n, at(dk=1))

    def pass_on(event):
        for s in (2 * event, 2 * event + 1):
            q_start(s)
        q_step(event, 2)

    send("Y", None, turned, slab(near(0), yhi), pair, at(dy=2))
    side(0, turned)
    my_head = head(near(0), yhi)
    for r in range(1, 8):
        send("R", row == 0, turned.at[0], my_head, head_own, (r, col))
    keep_slab = keep(turned, slab(near(0), yhi))
    keep_slab.start()
    keep_head = keep(turned.at[0], my_head)
    pl.when(row == 0)(lambda: keep_head.start())
    l_step(6)
    keep_slab.wait()
    q_start(0)
    l_step(7)
    arrive("Y", None, slab(near(0), 1 - yhi), pair)
    side(1, slab(near(0), 1 - yhi))
    q_start(1)
    pl.when(row == 0)(lambda: keep_head.wait())
    arrive("R", row != 0, my_head, head_own)
    send("R", None, my_head, my_head, head_partner, at(dy=2))
    q_step(0, 2)
    l_step(8)
    for n in range(2):
        arrive("K", None, slab(near(0, 1), halves[n]), core + n)
    pass_on(1)
    l_step(9)
    for n in range(2):
        into_halves(near(0), n)
        into_halves(near(0, 1), n)
    for h in range(2):
        for n, (source, dx) in enumerate(((right, 3), (left, 1))):
            here = slab(near(dx), halves[h])
            arrive("X", None, here, source + h)
            if n == h:
                send("X", None, here, here, far + h, at(dx=4 - dx))
            send("K", None, here, here, core + 2 + 2 * h + n, at(dk=1))
        pass_on(2 + 2 * h)
        if h == 0:
            arrive("R", None, head(near(0), 1 - yhi), head_partner)
            mid = head(near(0), 0, 2)
            send("R", None, mid, mid, h_right, at(dx=1))
            send("R", None, mid, mid, h_left, at(dx=3))
            send("R", None, mid, mid, h_core, at(dk=1))
        else:
            for n, (source, dx) in enumerate(((h_right, 3), (h_left, 1))):
                here = head(near(dx), 0, 2)
                arrive("R", None, here, source)
                if n == 0:
                    send("R", None, here, here, h_far, at(dx=1))
                send("R", None, here, here, h_core + 1 + n, at(dk=1))
        for n, dx in enumerate((3, 1)):
            arrive("K", None, slab(near(dx, 1), halves[h]), core + 2 + 2 * h + n)
        pass_on(3 + 2 * h)
        if h == 0:

            @pl.when(mine)
            def _():
                for copy in l_own:
                    copy.wait()

            l_take_over()
            for c in range(2):
                spread(lj.at[c], ljh.at[c], ljl.at[c])
        for dx in (3, 1):
            into_halves(near(dx), halves[h])
            into_halves(near(dx, 1), halves[h])
    for h in range(2):
        here = slab(near(2), halves[h])
        arrive("X", None, here, far + h)
        send("K", None, here, here, core + 6 + h, at(dk=1))
    pass_on(6)
    here = head(near(2), 0, 2)
    arrive("R", None, here, h_far)
    send("R", None, here, here, h_core + 3, at(dk=1))
    for h in range(2):
        arrive("K", None, slab(near(2, 1), halves[h]), core + 6 + h)
    pass_on(7)

    @pl.when(mine)
    def _():
        for copy in q_own:
            copy.start()

    saves = []

    def save(pairs):
        for src, dst in pairs:
            one = keep(src, dst)
            one.start()
            saves.append(one)

    @pl.when(row == 0)
    def _():
        lih[0] = jnp.zeros((nb, nb), BF)
        lil[0] = jnp.zeros((nb, nb), BF)

    save([(lih, lih_out), (lil, lil_out)])

    def put(b, c, values):
        for t in range(4):
            here = pl.ds(b * 8 * nb + c * 4 + t, nb, stride=8)
            blk[here, :] = values(here, t)

    def first_half(b):
        @pl.loop(0, 2)
        def _(c):
            side = jnp.logical_and(col == 0, c == 0)

            @pl.when(side)
            def _():
                put(b, c, lambda here, t: qi[b, :, t * 128 : (t + 1) * 128])

            @pl.when(jnp.logical_not(jnp.logical_or(side, row + b == 0)))
            def _():
                acc = dot3(qh[b], ql[b], ljh[c], ljl[c], NT)
                put(b, c, lambda here, t: blk[here, :] - acc[:, t * 128 : (t + 1) * 128])

    def save_block(b):
        here = pl.ds(b * 8 * nb, 8 * nb)
        save([(blk.at[here], a_out.at[here])])

    q_step(8, 2)
    for n in range(2):
        into_halves(near(2), n)
        into_halves(near(2, 1), n)
    load_blocks.wait()
    first_half(3)
    save_block(3)
    q_step(9, 2)
    for n, dx in enumerate((0, 3, 1, 2)):
        arrive("R", None, head(near(dx, 1), 0, 2), h_core + n)

    rh, rl = split(qi[4])
    cf[...] = dot3(dh[...], dl[...], rh, rl, NN)
    sh[...], sl[...] = split(0.5 * (cf[...] + cf[...].T))
    for b in (2, 1):
        first_half(b)
        save_block(b)
    l_finish()
    for c in range(2):
        lj[c] = dot3(ljh[c], ljl[c], sh[...], sl[...], NN)
    first_half(0)
    q_take_over()

    @pl.when(mine)
    def _():
        for copy in q_own:
            copy.wait()

    for c in range(2):

        @pl.loop(0, 8)
        def _(n):
            here = pl.ds(pl.multiple_of(n * (nb // 8), nb // 8), nb // 8)
            gh[c, here, :], gl[c, here, :] = split(qj[c, here, :] - lj[c, here, :])

        if c == 0:

            @pl.when(col == 0)
            def _():
                gh[0], gl[0] = split(cf[...].T)

        save([(gh.at[c], gh_out.at[c]), (gl.at[c], gl_out.at[c])])

    @pl.when(row == 0)
    def _():
        sh[...], sl[...] = split(cf[...])

        @pl.loop(0, 2)
        def _(c):
            fin = (qj[c] - dot3(ljh[c], ljl[c], sh[...], sl[...], NN)).T
            put(0, c, lambda here, t: fin[:, t * 128 : (t + 1) * 128])

        @pl.when(col == 0)
        def _():
            put(0, 0, lambda here, t: cf[:, t * 128 : (t + 1) * 128])

    save_block(0)
    q_finish()
    for cond, body in open_sends:
        when(cond, body)
    for one in saves:
        one.wait()
    assert used["send"] <= send_sems.shape[0], used
    assert used["recv"] <= recv_sems.shape[0], used
    assert used["local"] <= local_sems.shape[0], used


def gather(a, blocks, low, dinv):
    nb = dinv.shape[0]
    part = nb // PIECES
    anywhere = pl.BlockSpec(memory_space=pl.ANY)
    return pl.pallas_call(
        gather_kernel,
        out_shape=(
            jax.ShapeDtypeStruct(blocks.shape, F32),
            jax.ShapeDtypeStruct((4, nb, nb), BF),
            jax.ShapeDtypeStruct((4, nb, nb), BF),
            jax.ShapeDtypeStruct((2, nb, nb), BF),
            jax.ShapeDtypeStruct((2, nb, nb), BF),
        ),
        in_specs=[anywhere, anywhere, anywhere, pl.BlockSpec(memory_space=pltpu.VMEM)],
        out_specs=(anywhere,) * 5,
        scratch_shapes=[
            pltpu.VMEM((4, part, 4, 128), F32),
            pltpu.VMEM((4, part, nb), F32),
            pltpu.VMEM((nb, nb), BF),
            pltpu.VMEM((nb, nb), BF),
            pltpu.VMEM((4, nb, nb), F32),
            pltpu.VMEM((5, nb, nb), F32),
            pltpu.VMEM((2, nb, nb), F32),
            pltpu.VMEM((2, nb, nb), F32),
            pltpu.VMEM(blocks.shape, F32),
            pltpu.VMEM((4, nb, nb), BF),
            pltpu.VMEM((4, nb, nb), BF),
            pltpu.VMEM((4, nb, nb), BF),
            pltpu.VMEM((4, nb, nb), BF),
            pltpu.VMEM((2, nb, nb), BF),
            pltpu.VMEM((2, nb, nb), BF),
            pltpu.VMEM((2, nb, nb), BF),
            pltpu.VMEM((2, nb, nb), BF),
            pltpu.VMEM((nb, nb), F32),
            pltpu.VMEM((nb, nb), BF),
            pltpu.VMEM((nb, nb), BF),
            pltpu.SemaphoreType.DMA((280,)),
            pltpu.SemaphoreType.DMA((140,)),
            pltpu.SemaphoreType.DMA((32,)),
        ],
        compiler_params=pltpu.CompilerParams(
            collective_id=0, has_side_effects=True, vmem_limit_bytes=60 << 20
        ),
        name="gather",
    )(a, blocks, low, dinv)


def update_kernel(a, lh, ll, gh, gl, o):
    nb = lh.shape[1]

    @pl.loop(0, 2)
    def _(c):
        acc = dot3(lh[0], ll[0], gh[c], gl[c], NT)
        for t in range(4):
            here = pl.ds(c * 4 + t, nb, stride=8)
            o[here, :] = a[here, :] - acc[:, t * 128 : (t + 1) * 128]


def update(a, lh, ll, gh, gl):
    nb = lh.shape[1]
    pairs = pl.BlockSpec((2, nb, nb), lambda b: (0, 0, 0))
    block = pl.BlockSpec((1, nb, nb), lambda b: (b, 0, 0))
    linear = pl.BlockSpec((8 * nb, 128), lambda b: (b, 0))
    return pl.pallas_call(
        update_kernel,
        grid=(4,),
        out_shape=jax.ShapeDtypeStruct(a.shape, F32),
        in_specs=[linear, block, block, pairs, pairs],
        out_specs=linear,
        compiler_params=pltpu.CompilerParams(vmem_limit_bytes=56 << 20),
        name="update",
    )(a, lh, ll, gh, gl)


def body(stiffness, lower_panel, diag_inverse):
    tiles = stiffness.reshape(4, 512, 2, 4, 128)
    rows = stiffness.reshape(16384, 128)
    out = update(*gather(tiles, rows, lower_panel[:, 0], diag_inverse))
    return out.reshape(stiffness.shape)


def solution(mesh):
    in_specs = (P(None, "row", None, None, "col", None), P(None, "row", None, None), P())
    out_specs = P(None, "row", None, None, "col", None)
    return jax.shard_map(body, mesh=mesh, in_specs=in_specs, out_specs=out_specs, check_vma=False)
```

```python
import functools

import jax
import jax.numpy as jnp
from jax import lax
from jax.experimental import pallas as pl
from jax.experimental.pallas import tpu as pltpu
from jax.sharding import PartitionSpec as P

F32, BF = jnp.float32, jnp.bfloat16
MESH = pl.DeviceIdType.MESH
NT = (((1,), (1,)), ((), ()))
NN = (((1,), (0,)), ((), ()))
PIECES = 16
CHUNKS = 8


def split(x):
    high = x.astype(BF)
    return high, (x - high.astype(F32)).astype(BF)


def dot3(ah, al, bh, bl, dims):
    dot = functools.partial(
        lax.dot_general, dimension_numbers=dims, preferred_element_type=F32
    )
    return dot(ah, bh) + dot(ah, bl) + dot(al, bh)


def gather_kernel(
    a, blocks, low, dinv, a_out, lih_out, lil_out, gh_out, gl_out,
    raw, turned, dh, dl, li, qi, lj, qj, blk, qh, ql, lih, lil, ljh, ljl, gh, gl, cf, sh, sl,
    send_sems, recv_sems, local_sems,
):
    row, col = lax.axis_index("row"), lax.axis_index("col")
    z, ylo = row // 2, lax.rem(row, 2)
    yhi, x, k = col // 8, lax.rem(col // 2, 4), lax.rem(col, 2)
    y = 2 * yhi + ylo
    nb = dinv.shape[0]
    part = nb // PIECES

    def at(dx=0, dy=0, dz=0, dk=0):
        nx, ny = lax.rem(x + dx + 4, 4), lax.rem(y + dy + 4, 4)
        nz, nk = lax.rem(z + dz + 4, 4), lax.rem(k + dk, 2)
        return (2 * nz + lax.rem(ny, 2), 8 * (ny // 2) + 2 * nx + nk)

    used = {"send": 0, "recv": 0, "local": 0}
    open_sends = []

    def take(kind, count=1):
        first = used[kind]
        used[kind] += count
        return first

    def when(cond, body):
        if cond is None:
            body()
        else:
            pl.when(cond)(body)

    def tagged(tag, cond, body):
        when(cond, body)

    def send(tag, cond, src, dst, recv, device):
        sem = take("send")

        def copy():
            return pltpu.make_async_remote_copy(
                src_ref=src,
                dst_ref=dst,
                send_sem=send_sems.at[sem],
                recv_sem=recv_sems.at[recv],
                device_id=device,
                device_id_type=MESH,
            )

        when(cond, lambda: copy().start())
        open_sends.append((cond, lambda: copy().wait_send()))

    def arrive(tag, cond, dst, recv):
        def body():
            pltpu.make_async_remote_copy(
                src_ref=dst,
                dst_ref=dst,
                send_sem=send_sems.at[0],
                recv_sem=recv_sems.at[recv],
                device_id=at(dk=1),
                device_id_type=MESH,
            ).wait_recv()

        when(cond, body)

    def keep(src, dst):
        return pltpu.make_async_copy(src, dst, local_sems.at[take("local")])

    load_low = keep(low, li)
    load_low.start()
    load_blocks = keep(blocks, blk)
    load_blocks.start()
    barrier = pltpu.get_barrier_semaphore()

    def greet(cond, device):
        when(
            cond,
            lambda: pl.semaphore_signal(
                barrier, inc=1, device_id=device, device_id_type=MESH
            ),
        )

    neighbours = [at(dx=1), at(dx=3), at(dy=1), at(dy=3), at(dz=1), at(dz=3), at(dy=2), at(dk=1)]
    greet(col != 0, (row, 0))
    for device in neighbours:
        greet(None, device)
    greet(row != 0, (0, col))
    expect = (
        len(neighbours)
        + jnp.where(col == 0, PIECES - 1, 0)
        + jnp.where(row == 0, 7, 0)
    )
    pl.semaphore_wait(barrier, expect)

    def place(eighth, upper, count=1):
        return pl.ds(pl.multiple_of((2 * eighth + upper) * part, part), count * part)

    raw_recv = take("recv")
    for piece in (12, 10, 13, 11, 4, 2, 5, 3, 14, 8, 15, 9, 6, 1, 7):
        send(
            "S",
            col == 0,
            a.at[:, place(piece % 8, piece // 8), 0],
            raw,
            raw_recv,
            (row, piece),
        )
    own_raw = keep(a.at[:, place(0, 0), 0], raw)
    pl.when(col == 0)(lambda: own_raw.start())

    dz = lax.rem(z - x + 4, 4)
    chain = ylo == k
    mine = jnp.logical_and(dz == 0, chain)
    relays = jnp.logical_and(dz != 0, chain)
    hops = tuple(jnp.where(h == 3, 1, h) for h in (dz, lax.rem(4 - dz, 4)))
    passes = (dz == 1, dz == 3)
    up = (at(dz=1), at(dz=3))
    beside = at(dy=jnp.where(ylo == 0, 1, 3))

    def exchange(tag, source, target, chunks, rows):
        cross = take("recv", 2 * chunks)
        ring = take("recv", 2 * chunks)
        to_ring = take("send", 2 * chunks)
        to_cross = take("send", 2 * chunks)
        to_back = take("send", 2 * chunks)

        def move(src, here, sends, recvs, n, device):
            return pltpu.make_async_remote_copy(
                src_ref=src,
                dst_ref=here,
                send_sem=send_sems.at[sends + n],
                recv_sem=recv_sems.at[recvs + n],
                device_id=device,
                device_id_type=MESH,
            )

        def both_ways(c, s, src, here):
            n = c * chunks + s
            return (
                move(src, here, to_ring, ring, n, up[c]),
                move(src, here, to_cross, cross, n, beside),
            )

        def start(s):
            @pl.when(mine)
            def _():
                for c in range(2):
                    here = rows(s)
                    src, dst = source.at[2 * c + yhi, here], target.at[c, here]
                    for one in both_ways(c, s, src, dst):
                        one.start()
                    move(src, dst, to_back, ring, c * chunks + s, up[1 - c]).start()

        def step(t, group=1):
            for c in range(2):
                first = t - hops[c]
                live = jnp.logical_and(
                    relays, jnp.logical_and(first >= 0, first < chunks // group)
                )
                for e in range(group):
                    s = first * group + e
                    here = target.at[c, rows(s)]

                    @pl.when(live)
                    def _():
                        arrive(tag, None, here, ring + c * chunks + s)
                        onward, over = both_ways(c, s, here, here)
                        pl.when(passes[c])(lambda: onward.start())
                        over.start()

        def take_over():
            @pl.when(jnp.logical_not(chain))
            def _():
                @pl.loop(0, chunks)
                def _(s):
                    for c in range(2):
                        arrive(tag, None, target.at[c, rows(s)], cross + c * chunks + s)

        def finish():
            @pl.when(chain)
            def _():
                @pl.loop(0, chunks)
                def _(s):
                    for c in range(2):
                        here = target.at[c, rows(s)]
                        onward, over = both_ways(c, s, here, here)
                        n = c * chunks + s
                        pl.when(jnp.logical_or(mine, passes[c]))(lambda: onward.wait_send())
                        over.wait_send()
                        pl.when(mine)(
                            lambda: move(here, here, to_back, ring, n, up[1 - c]).wait_send()
                        )

        return start, step, take_over, finish

    def own_blocks(source, target):
        return [keep(source.at[2 * c + yhi], target.at[c]) for c in range(2)]

    size = nb // CHUNKS
    l_start, l_step, l_take_over, l_finish = exchange(
        "L", low, lj, CHUNKS, lambda s: pl.ds(pl.multiple_of(s * size, size), size)
    )
    l_own = own_blocks(low, lj)

    def slice_rows(s):
        group, other, e = s // 4, lax.rem(s // 2, 2), lax.rem(s, 2)
        ends = jnp.logical_or(group == 0, group == 3)
        second = jnp.where(ends, e, group - 1)
        upper = jnp.where(second == 0, yhi, 1 - yhi)
        dx = jnp.where(group == 0, 0, jnp.where(group == 3, 2, 3 - 2 * e))
        return place(2 * lax.rem(x + dx, 4) + lax.rem(k + other, 2), upper)

    q_start, q_step, q_take_over, q_finish = exchange("Q", qi, qj, PIECES, slice_rows)
    q_own = own_blocks(qi, qj)

    def spread(source, high, low_part, count=8):
        size = nb // count

        @pl.loop(0, count)
        def _(n):
            rows = pl.ds(pl.multiple_of(n * size, size), size)
            high[rows, :], low_part[rows, :] = split(source[rows, :])

    @pl.when(mine)
    def _():
        for copy in l_own:
            copy.start()

    for s in range(CHUNKS):
        l_start(s)
    dh[...], dl[...] = split(dinv[...])
    l_step(0)
    load_low.wait()
    for b in range(4):
        spread(li.at[b], lih.at[b], lil.at[b])
        l_step(1 + b)
    l_step(5)
    arrive("S", col != 0, raw, raw_recv)
    pl.when(col == 0)(lambda: own_raw.wait())

    rows = jnp.concatenate(
        [
            jnp.concatenate([raw[b, :, t, :] for t in range(4)], axis=1)
            for b in range(4)
        ],
        axis=0,
    )
    high, lo = split(rows)
    turned[...] = dot3(high, lo, dh[...], dl[...], NT).reshape(turned.shape)

    def near(dx, dk=0):
        return 2 * lax.rem(x + dx, 4) + lax.rem(k + dk, 2)

    halves = (yhi, 1 - yhi)

    def slab(eighth, upper):
        return qi.at[pl.ds(0, 4), place(eighth, upper)]

    def head(eighth, upper, count=1):
        return qi.at[4, place(eighth, upper, count)]

    def into_halves(eighth, upper):
        here = place(eighth, upper)

        @pl.loop(0, 4)
        def _(b):
            qh[b, here, :], ql[b, here, :] = split(qi[b, here, :])

    def first_half(eighth):
        pair_rows = place(eighth, 0, 2)
        count = 2 * part

        @pl.loop(0, 2)
        def _(c):
            side = jnp.logical_and(col == 0, c == 0)

            def put_rows(values):
                for b in range(4):
                    for t in range(4):
                        start = b * 8 * nb + 16 * eighth * part + c * 4 + t
                        here = pl.ds(start, count, stride=8)
                        blk[here, :] = values(here, b, slice(t * 128, (t + 1) * 128))

            @pl.when(side)
            def _():
                put_rows(lambda here, b, cols: qi[b, pair_rows, cols])

            @pl.when(jnp.logical_not(side))
            def _():
                high = qh[:, pair_rows, :].reshape(4 * count, nb)
                rest = ql[:, pair_rows, :].reshape(4 * count, nb)
                acc = dot3(high, rest, ljh[c], ljl[c], NT)
                put_rows(
                    lambda here, b, cols: blk[here, :] - acc[b * count : (b + 1) * count, cols]
                )

    right, left, far, core = take("recv", 2), take("recv", 2), take("recv", 2), take("recv", 8)
    pair, head_own, head_partner = take("recv"), take("recv"), take("recv")
    h_right, h_left, h_far, h_core = take("recv"), take("recv"), take("recv"), take("recv", 4)

    def side(n, src):
        here = slab(near(0), halves[n])
        send("X", None, src, here, right + n, at(dx=1))
        send("X", None, src, here, left + n, at(dx=3))
        send("K", None, src, here, core + n, at(dk=1))

    def pass_on(event):
        for s in (2 * event, 2 * event + 1):
            q_start(s)
        q_step(event, 2)

    send("Y", None, turned, slab(near(0), yhi), pair, at(dy=2))
    side(0, turned)
    my_head = head(near(0), yhi)
    for r in range(1, 8):
        send("R", row == 0, turned.at[0], my_head, head_own, (r, col))
    keep_slab = keep(turned, slab(near(0), yhi))
    keep_slab.start()
    keep_head = keep(turned.at[0], my_head)
    pl.when(row == 0)(lambda: keep_head.start())
    l_step(6)
    keep_slab.wait()
    q_start(0)
    l_step(7)
    arrive("Y", None, slab(near(0), 1 - yhi), pair)
    side(1, slab(near(0), 1 - yhi))
    q_start(1)
    pl.when(row == 0)(lambda: keep_head.wait())
    arrive("R", row != 0, my_head, head_own)
    send("R", None, my_head, my_head, head_partner, at(dy=2))
    q_step(0, 2)
    l_step(8)
    for n in range(2):
        arrive("K", None, slab(near(0, 1), halves[n]), core + n)
    pass_on(1)
    l_step(9)
    for n in range(2):
        into_halves(near(0), n)
        into_halves(near(0, 1), n)
    for h in range(2):
        for n, (source, dx) in enumerate(((right, 3), (left, 1))):
            here = slab(near(dx), halves[h])
            arrive("X", None, here, source + h)
            if n == h:
                send("X", None, here, here, far + h, at(dx=4 - dx))
            send("K", None, here, here, core + 2 + 2 * h + n, at(dk=1))
        pass_on(2 + 2 * h)
        if h == 0:
            arrive("R", None, head(near(0), 1 - yhi), head_partner)
            mid = head(near(0), 0, 2)
            send("R", None, mid, mid, h_right, at(dx=1))
            send("R", None, mid, mid, h_left, at(dx=3))
            send("R", None, mid, mid, h_core, at(dk=1))
        else:
            for n, (source, dx) in enumerate(((h_right, 3), (h_left, 1))):
                here = head(near(dx), 0, 2)
                arrive("R", None, here, source)
                if n == 0:
                    send("R", None, here, here, h_far, at(dx=1))
                send("R", None, here, here, h_core + 1 + n, at(dk=1))
        for n, dx in enumerate((3, 1)):
            arrive("K", None, slab(near(dx, 1), halves[h]), core + 2 + 2 * h + n)
        pass_on(3 + 2 * h)
        if h == 0:

            @pl.when(mine)
            def _():
                for copy in l_own:
                    copy.wait()

            l_take_over()
            for c in range(2):
                spread(lj.at[c], ljh.at[c], ljl.at[c])
            load_blocks.wait()
        for dx in (3, 1):
            into_halves(near(dx), halves[h])
            into_halves(near(dx, 1), halves[h])
        if h == 0:
            first_half(near(0))
            first_half(near(0, 1))
        else:
            for dx in (3, 1):
                first_half(near(dx))
                first_half(near(dx, 1))
    for h in range(2):
        here = slab(near(2), halves[h])
        arrive("X", None, here, far + h)
        send("K", None, here, here, core + 6 + h, at(dk=1))
    pass_on(6)
    here = head(near(2), 0, 2)
    arrive("R", None, here, h_far)
    send("R", None, here, here, h_core + 3, at(dk=1))
    for h in range(2):
        arrive("K", None, slab(near(2, 1), halves[h]), core + 6 + h)
    pass_on(7)

    @pl.when(mine)
    def _():
        for copy in q_own:
            copy.start()

    saves = []

    def save(pairs):
        for src, dst in pairs:
            one = keep(src, dst)
            one.start()
            saves.append(one)

    @pl.when(row == 0)
    def _():
        lih[0] = jnp.zeros((nb, nb), BF)
        lil[0] = jnp.zeros((nb, nb), BF)

    save([(lih, lih_out), (lil, lil_out)])

    def put(b, c, values):
        for t in range(4):
            here = pl.ds(b * 8 * nb + c * 4 + t, nb, stride=8)
            blk[here, :] = values(here, t)

    def save_block(b):
        here = pl.ds(b * 8 * nb, 8 * nb)
        save([(blk.at[here], a_out.at[here])])

    q_step(8, 2)
    for n in range(2):
        into_halves(near(2), n)
        into_halves(near(2, 1), n)
    first_half(near(2))
    first_half(near(2, 1))
    for b in range(1, 4):
        save_block(b)
    q_step(9, 2)
    for n, dx in enumerate((0, 3, 1, 2)):
        arrive("R", None, head(near(dx, 1), 0, 2), h_core + n)

    rh, rl = split(qi[4])
    cf[...] = dot3(dh[...], dl[...], rh, rl, NN)
    sh[...], sl[...] = split(0.5 * (cf[...] + cf[...].T))
    l_finish()
    for c in range(2):
        lj[c] = dot3(ljh[c], ljl[c], sh[...], sl[...], NN)
    q_take_over()

    @pl.when(mine)
    def _():
        for copy in q_own:
            copy.wait()

    for c in range(2):

        @pl.loop(0, 8)
        def _(n):
            here = pl.ds(pl.multiple_of(n * (nb // 8), nb // 8), nb // 8)
            gh[c, here, :], gl[c, here, :] = split(qj[c, here, :] - lj[c, here, :])

        if c == 0:

            @pl.when(col == 0)
            def _():
                gh[0], gl[0] = split(cf[...].T)

        save([(gh.at[c], gh_out.at[c]), (gl.at[c], gl_out.at[c])])

    @pl.when(row == 0)
    def _():
        sh[...], sl[...] = split(cf[...])

        @pl.loop(0, 2)
        def _(c):
            fin = (qj[c] - dot3(ljh[c], ljl[c], sh[...], sl[...], NN)).T
            put(0, c, lambda here, t: fin[:, t * 128 : (t + 1) * 128])

        @pl.when(col == 0)
        def _():
            put(0, 0, lambda here, t: cf[:, t * 128 : (t + 1) * 128])

    save_block(0)
    q_finish()
    for cond, body in open_sends:
        when(cond, body)
    for one in saves:
        one.wait()
    assert used["send"] <= send_sems.shape[0], used
    assert used["recv"] <= recv_sems.shape[0], used
    assert used["local"] <= local_sems.shape[0], used


def gather(a, blocks, low, dinv):
    nb = dinv.shape[0]
    part = nb // PIECES
    anywhere = pl.BlockSpec(memory_space=pl.ANY)
    return pl.pallas_call(
        gather_kernel,
        out_shape=(
            jax.ShapeDtypeStruct(blocks.shape, F32),
            jax.ShapeDtypeStruct((4, nb, nb), BF),
            jax.ShapeDtypeStruct((4, nb, nb), BF),
            jax.ShapeDtypeStruct((2, nb, nb), BF),
            jax.ShapeDtypeStruct((2, nb, nb), BF),
        ),
        in_specs=[anywhere, anywhere, anywhere, pl.BlockSpec(memory_space=pltpu.VMEM)],
        out_specs=(anywhere,) * 5,
        scratch_shapes=[
            pltpu.VMEM((4, part, 4, 128), F32),
            pltpu.VMEM((4, part, nb), F32),
            pltpu.VMEM((nb, nb), BF),
            pltpu.VMEM((nb, nb), BF),
            pltpu.VMEM((4, nb, nb), F32),
            pltpu.VMEM((5, nb, nb), F32),
            pltpu.VMEM((2, nb, nb), F32),
            pltpu.VMEM((2, nb, nb), F32),
            pltpu.VMEM(blocks.shape, F32),
            pltpu.VMEM((4, nb, nb), BF),
            pltpu.VMEM((4, nb, nb), BF),
            pltpu.VMEM((4, nb, nb), BF),
            pltpu.VMEM((4, nb, nb), BF),
            pltpu.VMEM((2, nb, nb), BF),
            pltpu.VMEM((2, nb, nb), BF),
            pltpu.VMEM((2, nb, nb), BF),
            pltpu.VMEM((2, nb, nb), BF),
            pltpu.VMEM((nb, nb), F32),
            pltpu.VMEM((nb, nb), BF),
            pltpu.VMEM((nb, nb), BF),
            pltpu.SemaphoreType.DMA((280,)),
            pltpu.SemaphoreType.DMA((140,)),
            pltpu.SemaphoreType.DMA((32,)),
        ],
        compiler_params=pltpu.CompilerParams(
            collective_id=0, has_side_effects=True, vmem_limit_bytes=60 << 20
        ),
        name="gather",
    )(a, blocks, low, dinv)


def update_kernel(a, lh, ll, gh, gl, o):
    nb = lh.shape[1]

    half = nb // 2
    for n in range(4):
        cols = pl.ds(n % 2 * half, half)
        acc = dot3(lh[0], ll[0], gh[n // 2, cols], gl[n // 2, cols], NT)
        for t in range(2):
            here = pl.ds(n * 2 + t, nb, stride=8)
            o[here, :] = a[here, :] - acc[:, t * 128 : (t + 1) * 128]


def update(a, lh, ll, gh, gl):
    nb = lh.shape[1]
    pairs = pl.BlockSpec((2, nb, nb), lambda b: (0, 0, 0))
    block = pl.BlockSpec((1, nb, nb), lambda b: (b, 0, 0))
    linear = pl.BlockSpec((8 * nb, 128), lambda b: (b, 0))
    return pl.pallas_call(
        update_kernel,
        grid=(4,),
        out_shape=jax.ShapeDtypeStruct(a.shape, F32),
        in_specs=[linear, block, block, pairs, pairs],
        out_specs=linear,
        compiler_params=pltpu.CompilerParams(vmem_limit_bytes=56 << 20),
        name="update",
    )(a, lh, ll, gh, gl)


def body(stiffness, lower_panel, diag_inverse):
    tiles = stiffness.reshape(4, 512, 2, 4, 128)
    rows = stiffness.reshape(16384, 128)
    out = update(*gather(tiles, rows, lower_panel[:, 0], diag_inverse))
    return out.reshape(stiffness.shape)


def solution(mesh):
    in_specs = (P(None, "row", None, None, "col", None), P(None, "row", None, None), P())
    out_specs = P(None, "row", None, None, "col", None)
    return jax.shard_map(body, mesh=mesh, in_specs=in_specs, out_specs=out_specs, check_vma=False)
```

```python
import functools

import jax
import jax.numpy as jnp
from jax import lax
from jax.experimental import pallas as pl
from jax.experimental.pallas import tpu as pltpu
from jax.sharding import PartitionSpec as P

F32, BF = jnp.float32, jnp.bfloat16
MESH = pl.DeviceIdType.MESH
NT = (((1,), (1,)), ((), ()))
NN = (((1,), (0,)), ((), ()))
PIECES = 16
CHUNKS = 8


def split(x):
    high = x.astype(BF)
    return high, (x - high.astype(F32)).astype(BF)


def dot3(ah, al, bh, bl, dims):
    dot = functools.partial(
        lax.dot_general, dimension_numbers=dims, preferred_element_type=F32
    )
    return dot(ah, bh) + dot(ah, bl) + dot(al, bh)


def gather_kernel(
    a, blocks, low, dinv_in, a_out, lih_out, lil_out, gh_out, gl_out,
    dinv, raw, turned, dh, dl, li, qi, lj, qj, blk, qh, ql, lih, lil, ljh, ljl, gh, gl, cf, sh, sl,
    send_sems, recv_sems, local_sems,
):
    row, col = lax.axis_index("row"), lax.axis_index("col")
    z, ylo = row // 2, lax.rem(row, 2)
    yhi, x, k = col // 8, lax.rem(col // 2, 4), lax.rem(col, 2)
    y = 2 * yhi + ylo
    nb = dinv.shape[0]
    part = nb // PIECES

    def at(dx=0, dy=0, dz=0, dk=0):
        nx, ny = lax.rem(x + dx + 4, 4), lax.rem(y + dy + 4, 4)
        nz, nk = lax.rem(z + dz + 4, 4), lax.rem(k + dk, 2)
        return (2 * nz + lax.rem(ny, 2), 8 * (ny // 2) + 2 * nx + nk)

    used = {"send": 0, "recv": 0, "local": 0}
    open_sends = []

    def take(kind, count=1):
        first = used[kind]
        used[kind] += count
        return first

    def when(cond, body):
        if cond is None:
            body()
        else:
            pl.when(cond)(body)

    def tagged(tag, cond, body):
        when(cond, body)

    def send(tag, cond, src, dst, recv, device):
        sem = take("send")

        def copy():
            return pltpu.make_async_remote_copy(
                src_ref=src,
                dst_ref=dst,
                send_sem=send_sems.at[sem],
                recv_sem=recv_sems.at[recv],
                device_id=device,
                device_id_type=MESH,
            )

        when(cond, lambda: copy().start())
        open_sends.append((cond, lambda: copy().wait_send()))

    def arrive(tag, cond, dst, recv):
        def body():
            pltpu.make_async_remote_copy(
                src_ref=dst,
                dst_ref=dst,
                send_sem=send_sems.at[0],
                recv_sem=recv_sems.at[recv],
                device_id=at(dk=1),
                device_id_type=MESH,
            ).wait_recv()

        when(cond, body)

    def keep(src, dst):
        return pltpu.make_async_copy(src, dst, local_sems.at[take("local")])

    load_dinv = keep(dinv_in, dinv)
    load_dinv.start()
    load_low = keep(low, li)
    load_low.start()
    load_blocks = keep(blocks, blk)
    load_blocks.start()
    barrier = pltpu.get_barrier_semaphore()

    def greet(cond, device):
        when(
            cond,
            lambda: pl.semaphore_signal(
                barrier, inc=1, device_id=device, device_id_type=MESH
            ),
        )

    neighbours = [at(dx=1), at(dx=3), at(dy=1), at(dy=3), at(dz=1), at(dz=3), at(dy=2), at(dk=1)]
    greet(col != 0, (row, 0))
    for device in neighbours:
        greet(None, device)
    greet(row != 0, (0, col))
    expect = (
        len(neighbours)
        + jnp.where(col == 0, PIECES - 1, 0)
        + jnp.where(row == 0, 7, 0)
    )
    pl.semaphore_wait(barrier, expect)

    def place(eighth, upper, count=1):
        return pl.ds(pl.multiple_of((2 * eighth + upper) * part, part), count * part)

    raw_recv = take("recv")
    for piece in (12, 10, 13, 11, 4, 2, 5, 3, 14, 8, 15, 9, 6, 1, 7):
        send(
            "S",
            col == 0,
            a.at[:, place(piece % 8, piece // 8), 0],
            raw,
            raw_recv,
            (row, piece),
        )
    own_raw = keep(a.at[:, place(0, 0), 0], raw)
    pl.when(col == 0)(lambda: own_raw.start())

    dz = lax.rem(z - x + 4, 4)
    chain = ylo == k
    mine = jnp.logical_and(dz == 0, chain)
    relays = jnp.logical_and(dz != 0, chain)
    hops = tuple(jnp.where(h == 3, 1, h) for h in (dz, lax.rem(4 - dz, 4)))
    passes = (dz == 1, dz == 3)
    up = (at(dz=1), at(dz=3))
    beside = at(dy=jnp.where(ylo == 0, 1, 3))

    def exchange(tag, source, target, chunks, rows):
        cross = take("recv", 2 * chunks)
        ring = take("recv", 2 * chunks)
        to_ring = take("send", 2 * chunks)
        to_cross = take("send", 2 * chunks)
        to_back = take("send", 2 * chunks)

        def move(src, here, sends, recvs, n, device):
            return pltpu.make_async_remote_copy(
                src_ref=src,
                dst_ref=here,
                send_sem=send_sems.at[sends + n],
                recv_sem=recv_sems.at[recvs + n],
                device_id=device,
                device_id_type=MESH,
            )

        def both_ways(c, s, src, here):
            n = c * chunks + s
            return (
                move(src, here, to_ring, ring, n, up[c]),
                move(src, here, to_cross, cross, n, beside),
            )

        def start(s):
            @pl.when(mine)
            def _():
                for c in range(2):
                    here = rows(s)
                    src, dst = source.at[2 * c + yhi, here], target.at[c, here]
                    for one in both_ways(c, s, src, dst):
                        one.start()
                    move(src, dst, to_back, ring, c * chunks + s, up[1 - c]).start()

        def step(t, group=1):
            for c in range(2):
                first = t - hops[c]
                live = jnp.logical_and(
                    relays, jnp.logical_and(first >= 0, first < chunks // group)
                )
                for e in range(group):
                    s = first * group + e
                    here = target.at[c, rows(s)]

                    @pl.when(live)
                    def _():
                        arrive(tag, None, here, ring + c * chunks + s)
                        onward, over = both_ways(c, s, here, here)
                        pl.when(passes[c])(lambda: onward.start())
                        over.start()

        def take_over():
            @pl.when(jnp.logical_not(chain))
            def _():
                @pl.loop(0, chunks)
                def _(s):
                    for c in range(2):
                        arrive(tag, None, target.at[c, rows(s)], cross + c * chunks + s)

        def finish():
            @pl.when(chain)
            def _():
                @pl.loop(0, chunks)
                def _(s):
                    for c in range(2):
                        here = target.at[c, rows(s)]
                        onward, over = both_ways(c, s, here, here)
                        n = c * chunks + s
                        pl.when(jnp.logical_or(mine, passes[c]))(lambda: onward.wait_send())
                        over.wait_send()
                        pl.when(mine)(
                            lambda: move(here, here, to_back, ring, n, up[1 - c]).wait_send()
                        )

        return start, step, take_over, finish

    def own_blocks(source, target):
        return [keep(source.at[2 * c + yhi], target.at[c]) for c in range(2)]

    size = nb // CHUNKS
    l_start, l_step, l_take_over, l_finish = exchange(
        "L", low, lj, CHUNKS, lambda s: pl.ds(pl.multiple_of(s * size, size), size)
    )
    l_own = own_blocks(low, lj)

    def slice_rows(s):
        group, other, e = s // 4, lax.rem(s // 2, 2), lax.rem(s, 2)
        ends = jnp.logical_or(group == 0, group == 3)
        second = jnp.where(ends, e, group - 1)
        upper = jnp.where(second == 0, yhi, 1 - yhi)
        dx = jnp.where(group == 0, 0, jnp.where(group == 3, 2, 3 - 2 * e))
        return place(2 * lax.rem(x + dx, 4) + lax.rem(k + other, 2), upper)

    q_start, q_step, q_take_over, q_finish = exchange("Q", qi, qj, PIECES, slice_rows)
    q_own = own_blocks(qi, qj)

    def spread(source, high, low_part, count=8):
        size = nb // count

        @pl.loop(0, count)
        def _(n):
            rows = pl.ds(pl.multiple_of(n * size, size), size)
            high[rows, :], low_part[rows, :] = split(source[rows, :])

    @pl.when(mine)
    def _():
        for copy in l_own:
            copy.start()

    for s in range(CHUNKS):
        l_start(s)
    load_dinv.wait()
    dh[...], dl[...] = split(dinv[...])
    l_step(0)
    load_low.wait()
    for b in range(4):
        spread(li.at[b], lih.at[b], lil.at[b])
        l_step(1 + b)
    l_step(5)
    arrive("S", col != 0, raw, raw_recv)
    pl.when(col == 0)(lambda: own_raw.wait())

    rows = jnp.concatenate(
        [
            jnp.concatenate([raw[b, :, t, :] for t in range(4)], axis=1)
            for b in range(4)
        ],
        axis=0,
    )
    high, lo = split(rows)
    turned[...] = dot3(high, lo, dh[...], dl[...], NT).reshape(turned.shape)

    def near(dx, dk=0):
        return 2 * lax.rem(x + dx, 4) + lax.rem(k + dk, 2)

    halves = (yhi, 1 - yhi)

    def slab(eighth, upper):
        return qi.at[pl.ds(0, 4), place(eighth, upper)]

    def head(eighth, upper, count=1):
        return qi.at[4, place(eighth, upper, count)]

    def into_halves(eighth, upper):
        here = place(eighth, upper)

        @pl.loop(0, 4)
        def _(b):
            qh[b, here, :], ql[b, here, :] = split(qi[b, here, :])

    def first_half(eighth):
        pair_rows = place(eighth, 0, 2)
        count = 2 * part

        @pl.loop(0, 2)
        def _(c):
            side = jnp.logical_and(col == 0, c == 0)

            def put_rows(values):
                for b in range(4):
                    for t in range(4):
                        start = b * 8 * nb + 16 * eighth * part + c * 4 + t
                        here = pl.ds(start, count, stride=8)
                        blk[here, :] = values(here, b, slice(t * 128, (t + 1) * 128))

            @pl.when(side)
            def _():
                put_rows(lambda here, b, cols: qi[b, pair_rows, cols])

            @pl.when(jnp.logical_not(side))
            def _():
                high = qh[:, pair_rows, :].reshape(4 * count, nb)
                rest = ql[:, pair_rows, :].reshape(4 * count, nb)
                acc = dot3(high, rest, ljh[c], ljl[c], NT)
                put_rows(
                    lambda here, b, cols: blk[here, :] - acc[b * count : (b + 1) * count, cols]
                )

    right, left, far, core = take("recv", 2), take("recv", 2), take("recv", 2), take("recv", 8)
    pair, head_own, head_partner = take("recv"), take("recv"), take("recv")
    h_right, h_left, h_far, h_core = take("recv"), take("recv"), take("recv"), take("recv", 4)

    def side(n, src):
        here = slab(near(0), halves[n])
        send("X", None, src, here, right + n, at(dx=1))
        send("X", None, src, here, left + n, at(dx=3))
        send("K", None, src, here, core + n, at(dk=1))

    def pass_on(event):
        for s in (2 * event, 2 * event + 1):
            q_start(s)
        q_step(event, 2)

    send("Y", None, turned, slab(near(0), yhi), pair, at(dy=2))
    side(0, turned)
    my_head = head(near(0), yhi)
    for r in range(1, 8):
        send("R", row == 0, turned.at[0], my_head, head_own, (r, col))
    keep_slab = keep(turned, slab(near(0), yhi))
    keep_slab.start()
    keep_head = keep(turned.at[0], my_head)
    pl.when(row == 0)(lambda: keep_head.start())
    l_step(6)
    keep_slab.wait()
    q_start(0)
    l_step(7)
    arrive("Y", None, slab(near(0), 1 - yhi), pair)
    side(1, slab(near(0), 1 - yhi))
    q_start(1)
    pl.when(row == 0)(lambda: keep_head.wait())
    arrive("R", row != 0, my_head, head_own)
    send("R", None, my_head, my_head, head_partner, at(dy=2))
    q_step(0, 2)
    l_step(8)
    for n in range(2):
        arrive("K", None, slab(near(0, 1), halves[n]), core + n)
    pass_on(1)
    l_step(9)
    for n in range(2):
        into_halves(near(0), n)
        into_halves(near(0, 1), n)
    for h in range(2):
        for n, (source, dx) in enumerate(((right, 3), (left, 1))):
            here = slab(near(dx), halves[h])
            arrive("X", None, here, source + h)
            if n == h:
                send("X", None, here, here, far + h, at(dx=4 - dx))
            send("K", None, here, here, core + 2 + 2 * h + n, at(dk=1))
        pass_on(2 + 2 * h)
        if h == 0:
            arrive("R", None, head(near(0), 1 - yhi), head_partner)
            mid = head(near(0), 0, 2)
            send("R", None, mid, mid, h_right, at(dx=1))
            send("R", None, mid, mid, h_left, at(dx=3))
            send("R", None, mid, mid, h_core, at(dk=1))
        else:
            for n, (source, dx) in enumerate(((h_right, 3), (h_left, 1))):
                here = head(near(dx), 0, 2)
                arrive("R", None, here, source)
                if n == 0:
                    send("R", None, here, here, h_far, at(dx=1))
                send("R", None, here, here, h_core + 1 + n, at(dk=1))
        for n, dx in enumerate((3, 1)):
            arrive("K", None, slab(near(dx, 1), halves[h]), core + 2 + 2 * h + n)
        pass_on(3 + 2 * h)
        if h == 0:

            @pl.when(mine)
            def _():
                for copy in l_own:
                    copy.wait()

            l_take_over()
            for c in range(2):
                spread(lj.at[c], ljh.at[c], ljl.at[c])
            load_blocks.wait()
        for dx in (3, 1):
            into_halves(near(dx), halves[h])
            into_halves(near(dx, 1), halves[h])
        if h == 0:
            first_half(near(0))
            first_half(near(0, 1))
        else:
            for dx in (3, 1):
                first_half(near(dx))
                first_half(near(dx, 1))
    for h in range(2):
        here = slab(near(2), halves[h])
        arrive("X", None, here, far + h)
        send("K", None, here, here, core + 6 + h, at(dk=1))
    pass_on(6)
    here = head(near(2), 0, 2)
    arrive("R", None, here, h_far)
    send("R", None, here, here, h_core + 3, at(dk=1))
    for h in range(2):
        arrive("K", None, slab(near(2, 1), halves[h]), core + 6 + h)
    pass_on(7)

    @pl.when(mine)
    def _():
        for copy in q_own:
            copy.start()

    saves = []

    def save(pairs):
        for src, dst in pairs:
            one = keep(src, dst)
            one.start()
            saves.append(one)

    @pl.when(row == 0)
    def _():
        lih[0] = jnp.zeros((nb, nb), BF)
        lil[0] = jnp.zeros((nb, nb), BF)

    save([(lih, lih_out), (lil, lil_out)])

    def put(b, c, values):
        for t in range(4):
            here = pl.ds(b * 8 * nb + c * 4 + t, nb, stride=8)
            blk[here, :] = values(here, t)

    def save_block(b):
        here = pl.ds(b * 8 * nb, 8 * nb)
        save([(blk.at[here], a_out.at[here])])

    q_step(8, 2)
    for n in range(2):
        into_halves(near(2), n)
        into_halves(near(2, 1), n)
    first_half(near(2))
    first_half(near(2, 1))
    for b in range(1, 4):
        save_block(b)
    first_rows = pl.ds(0, 8 * nb)
    save_first = keep(blk.at[first_rows], a_out.at[first_rows])
    pl.when(row != 0)(save_first.start)
    q_step(9, 2)
    for n, dx in enumerate((0, 3, 1, 2)):
        arrive("R", None, head(near(dx, 1), 0, 2), h_core + n)

    rh, rl = split(qi[4])
    cf[...] = dot3(dh[...], dl[...], rh, rl, NN)
    sh[...], sl[...] = split(0.5 * (cf[...] + cf[...].T))
    l_finish()
    for c in range(2):
        lj[c] = dot3(ljh[c], ljl[c], sh[...], sl[...], NN)
    q_take_over()

    @pl.when(mine)
    def _():
        for copy in q_own:
            copy.wait()

    for c in range(2):

        @pl.loop(0, 8)
        def _(n):
            here = pl.ds(pl.multiple_of(n * (nb // 8), nb // 8), nb // 8)
            gh[c, here, :], gl[c, here, :] = split(qj[c, here, :] - lj[c, here, :])

        if c == 0:

            @pl.when(col == 0)
            def _():
                gh[0], gl[0] = split(cf[...].T)

        save([(gh.at[c], gh_out.at[c]), (gl.at[c], gl_out.at[c])])

    @pl.when(row == 0)
    def _():
        sh[...], sl[...] = split(cf[...])

        @pl.loop(0, 2)
        def _(c):
            fin = (qj[c] - dot3(ljh[c], ljl[c], sh[...], sl[...], NN)).T
            put(0, c, lambda here, t: fin[:, t * 128 : (t + 1) * 128])

        @pl.when(col == 0)
        def _():
            put(0, 0, lambda here, t: cf[:, t * 128 : (t + 1) * 128])

    pl.when(row == 0)(save_first.start)
    save_first.wait()
    q_finish()
    for cond, body in open_sends:
        when(cond, body)
    for one in saves:
        one.wait()
    assert used["send"] <= send_sems.shape[0], used
    assert used["recv"] <= recv_sems.shape[0], used
    assert used["local"] <= local_sems.shape[0], used


def gather(a, blocks, low, dinv):
    nb = dinv.shape[0]
    part = nb // PIECES
    anywhere = pl.BlockSpec(memory_space=pl.ANY)
    return pl.pallas_call(
        gather_kernel,
        out_shape=(
            jax.ShapeDtypeStruct(blocks.shape, F32),
            jax.ShapeDtypeStruct((4, nb, nb), BF),
            jax.ShapeDtypeStruct((4, nb, nb), BF),
            jax.ShapeDtypeStruct((2, nb, nb), BF),
            jax.ShapeDtypeStruct((2, nb, nb), BF),
        ),
        in_specs=[anywhere] * 4,
        out_specs=(anywhere,) * 5,
        scratch_shapes=[
            pltpu.VMEM((nb, nb), F32),
            pltpu.VMEM((4, part, 4, 128), F32),
            pltpu.VMEM((4, part, nb), F32),
            pltpu.VMEM((nb, nb), BF),
            pltpu.VMEM((nb, nb), BF),
            pltpu.VMEM((4, nb, nb), F32),
            pltpu.VMEM((5, nb, nb), F32),
            pltpu.VMEM((2, nb, nb), F32),
            pltpu.VMEM((2, nb, nb), F32),
            pltpu.VMEM(blocks.shape, F32),
            pltpu.VMEM((4, nb, nb), BF),
            pltpu.VMEM((4, nb, nb), BF),
            pltpu.VMEM((4, nb, nb), BF),
            pltpu.VMEM((4, nb, nb), BF),
            pltpu.VMEM((2, nb, nb), BF),
            pltpu.VMEM((2, nb, nb), BF),
            pltpu.VMEM((2, nb, nb), BF),
            pltpu.VMEM((2, nb, nb), BF),
            pltpu.VMEM((nb, nb), F32),
            pltpu.VMEM((nb, nb), BF),
            pltpu.VMEM((nb, nb), BF),
            pltpu.SemaphoreType.DMA((280,)),
            pltpu.SemaphoreType.DMA((140,)),
            pltpu.SemaphoreType.DMA((32,)),
        ],
        compiler_params=pltpu.CompilerParams(
            collective_id=0, has_side_effects=True, vmem_limit_bytes=60 << 20
        ),
        name="gather",
    )(a, blocks, low, dinv)


def update_kernel(a, lh, ll, gh, gl, o):
    nb = lh.shape[1]

    half = nb // 2
    for n in range(4):
        cols = pl.ds(n % 2 * half, half)
        acc = dot3(lh[0], ll[0], gh[n // 2, cols], gl[n // 2, cols], NT)
        for t in range(2):
            here = pl.ds(n * 2 + t, nb, stride=8)
            o[here, :] = a[here, :] - acc[:, t * 128 : (t + 1) * 128]


def update(a, lh, ll, gh, gl):
    nb = lh.shape[1]
    pairs = pl.BlockSpec((2, nb, nb), lambda b: (0, 0, 0))
    block = pl.BlockSpec((1, nb, nb), lambda b: (b, 0, 0))
    linear = pl.BlockSpec((8 * nb, 128), lambda b: (b, 0))
    return pl.pallas_call(
        update_kernel,
        grid=(4,),
        out_shape=jax.ShapeDtypeStruct(a.shape, F32),
        in_specs=[linear, block, block, pairs, pairs],
        out_specs=linear,
        compiler_params=pltpu.CompilerParams(vmem_limit_bytes=56 << 20),
        name="update",
    )(a, lh, ll, gh, gl)


def body(stiffness, lower_panel, diag_inverse):
    tiles = stiffness.reshape(4, 512, 2, 4, 128)
    rows = stiffness.reshape(16384, 128)
    out = update(*gather(tiles, rows, lower_panel[:, 0], diag_inverse))
    return out.reshape(stiffness.shape)


def solution(mesh):
    in_specs = (P(None, "row", None, None, "col", None), P(None, "row", None, None), P())
    out_specs = P(None, "row", None, None, "col", None)
    return jax.shard_map(body, mesh=mesh, in_specs=in_specs, out_specs=out_specs, check_vma=False)
```
